128 devices in a mesh: dev: 128 (over x, y, z, core).
Axes of the slice: x: 4, y: 4, z: 4, core: 2. Of those that a mesh axis runs over, the one named last changes fastest.
Arguments:
- density: bfloat16 [1024, 262144], P('dev'), may hold values from -6 to 6
- flags: int32 [1024], P('dev'), may hold values 0 or 1
- courant: float32 [1024], P('dev'), may hold values from 0.1 to 0.9
- spectral: bfloat16 [1024, 1024], replicated, may hold values from -0.1875 to 0.1875
- tensor: bfloat16 [128, 1024, 1024], P('dev'), may hold values from -0.1875 to 0.1875
- owner: int32 [4], replicated, may hold values from 0 to 127, as said below
Outputs:
- coeffs: bfloat16 [1024, 262144], P(None, 'dev')
- collision: float32 [4, 262144], P(None, 'dev')
The draws below stay inside these ranges and needn't reach their ends.
Inputs may be any that keep to these rules, and one draw needn't show every extreme that they name: `owner`: distinct slice indices, one of which is 127.
All inputs are finite; a program needn't handle non-finite values. No bound on the sum of `flags` on one device may be relied on, other than what follows from the above.
Results may differ from the reference program's by a relative error of at most 0.0064.
Values may be sent and summed in bfloat16 or wider, within the bound.
No kernel may reach another device: no remote copies, remote signals or barrier semaphores. Data moves between devices by JAX's collectives and lax.ppermute only.
A program may use at most 128 MiB of HBM per device.

```python
import math
import jax
import jax.numpy as jnp
from jax import lax

V = 1024
K = 1024
NOUT = 4
CELLS = 262144
TABLE = 128


def draw_owner(key, part):
    first_key = jax.random.fold_in(key, 11)
    second_key = jax.random.fold_in(key, 23)
    others = jax.random.permutation(first_key, TABLE - 1)[:NOUT - 1].astype(jnp.int32)
    values = jnp.concatenate([jnp.full((1,), TABLE - 1, dtype=jnp.int32), others])
    order = jax.random.permutation(second_key, NOUT)
    return values[order].astype(jnp.int32)


def touch_ends(drawn, rng, least, high):
    longest = drawn.shape.index(max(drawn.shape))
    spots = []
    for shift in (0, 1):
        where = [jax.random.randint(jax.random.fold_in(rng, axis), (), 0, length) for axis, length in enumerate(drawn.shape)]
        where[longest] = (where[longest] + shift) % drawn.shape[longest]
        spots.append(tuple(where))
    return drawn.at[spots[0]].set(least).at[spots[1]].set(high)


def levels(key, extent, pieces, least, top_value):
    level, own = 1.0, jax.random.fold_in(key, 6)
    for position, parts in pieces:
        draws = jnp.exp(jax.random.uniform(jax.random.fold_in(own, position), (parts,), jnp.float32, least / len(pieces), top_value / len(pieces)))
        level = level * jnp.repeat(draws, extent[position] // parts).reshape([-1 if axis == position else 1 for axis in range(len(extent))])
    return level


def noise(own_key, shape, spread, most, shards=(), held_as=jnp.bfloat16):
    values = spread * jax.random.normal(own_key, shape, jnp.float32)
    if shards:
        values = values * levels(own_key, shape, shards, -0.22, 0.18)
    return jnp.clip(values, -most, most).astype(held_as)


def setup_inputs(seed: int = 0) -> dict:
    seeds = jax.random.split(jax.random.key(seed), 7)
    density = noise(seeds[0], (V, CELLS), 1.0, 6.0, ((0, 128),))
    flags = touch_ends((jax.random.randint(seeds[1], (V,), 0, 2) < 1).astype(jnp.int32), jax.random.fold_in(seeds[1], 1), 0, 1)
    courant = jnp.clip(jnp.exp(math.log(0.9) - 2.1972245 * jax.random.uniform(seeds[2], (V,), jnp.float32) ** levels(seeds[2], (V,), ((0, 128),), -0.2, 0.2)), 0.1, 0.9)
    spectral = noise(seeds[3], (K, V), V ** -0.5, 0.1875)
    tensor = noise(seeds[4], (TABLE, K, K), K ** -0.5, 0.1875, ((0, 128),))
    owner = draw_owner(jax.random.fold_in(seeds[6], 71), 0)
    return {"density": density, "flags": flags, "courant": courant, "spectral": spectral, "tensor": tensor, "owner": owner}


def reference(density, flags, courant, spectral, tensor, owner):
    field = density.astype(jnp.float32)
    upwind = jnp.where(flags[:, None] == 1, jnp.roll(field, 1, axis=1), jnp.roll(field, -1, axis=1))
    advected = (field - courant[:, None] * (field - upwind)).astype(jnp.bfloat16)
    coeffs = jnp.dot(spectral, advected, preferred_element_type=jnp.float32).astype(jnp.bfloat16)
    block = 8192 if CELLS % 8192 == 0 else CELLS
    count = CELLS // block
    rows = []
    for m in range(NOUT):
        slab = tensor[owner[m]]

        def per_block(index):
            part = lax.dynamic_slice_in_dim(coeffs, (index * block).astype(jnp.int32), block, 1)
            image = jnp.dot(slab, part, preferred_element_type=jnp.float32)
            return lax.optimization_barrier(jnp.sum(part.astype(jnp.float32) * image, axis=0)) / math.sqrt(K)
        rows.append(lax.map(per_block, jnp.arange(count, dtype=jnp.int32)).reshape(CELLS))
    return (coeffs, jnp.stack(rows))
```

```python
import math

import jax
import jax.numpy as jnp
from jax import lax
from jax.experimental import pallas as pl
from jax.experimental.pallas import tpu as pltpu
from jax.sharding import PartitionSpec as P

BLOCK = 256
LANES = 128
GROUP = 8


def fold_pairs(count):
    return [(i, j) for i in range(count) for j in range(i, count)]


def fold_kernel(t_ref, u_ref):
    count = t_ref.shape[1] // BLOCK
    for at, (i, j) in enumerate(fold_pairs(count)):
        rows, cols = pl.ds(i * BLOCK, BLOCK), pl.ds(j * BLOCK, BLOCK)
        block = t_ref[0, rows, cols]
        if i != j:
            mirror = t_ref[0, cols, rows].astype(jnp.float32).T
            block = (block.astype(jnp.float32) + mirror).astype(jnp.bfloat16)
        for half in range(BLOCK // LANES):
            start = (at * (BLOCK // LANES) + half) * BLOCK
            u_ref[pl.ds(start, BLOCK), :] = block[:, half * LANES : (half + 1) * LANES]


def fold(tensor):
    size = tensor.shape[1]
    rows = len(fold_pairs(size // BLOCK)) * BLOCK * (BLOCK // LANES)
    return pl.pallas_call(
        fold_kernel,
        out_shape=jax.ShapeDtypeStruct((rows, LANES), jnp.bfloat16),
        in_specs=[pl.BlockSpec(memory_space=pltpu.VMEM)],
        out_specs=pl.BlockSpec(memory_space=pltpu.VMEM),
        compiler_params=pltpu.CompilerParams(vmem_limit_bytes=24 << 20),
        cost_estimate=pl.CostEstimate(flops=2 * size * size, bytes_accessed=4 * size * size, transcendentals=0),
        name="fold",
    )(tensor)


def advect_kernel(flags_ref, courant_ref, before_ref, here_ref, after_ref, out_ref):
    nodes, width = out_ref.shape[1], out_ref.shape[2]
    row = lax.broadcasted_iota(jnp.int32, (nodes, 1), 0)
    flag = jnp.zeros((nodes, 1), jnp.int32)
    rate = jnp.zeros((nodes, 1), jnp.float32)
    for r in range(nodes):
        flag = jnp.where(row == r, flags_ref[r], flag)
        rate = jnp.where(row == r, courant_ref[r], rate)
    upward = jnp.broadcast_to(flag, (nodes, width)) == 1
    for d in range(out_ref.shape[0]):
        start, stop = d * width, (d + 1) * width
        last = d == out_ref.shape[0] - 1
        before = before_ref[...] if d == 0 else here_ref[:, start - LANES : start]
        after = after_ref[...] if last else here_ref[:, stop : stop + LANES]
        field = here_ref[:, start:stop].astype(jnp.float32)
        line = jnp.concatenate([before.astype(jnp.float32), field, after.astype(jnp.float32)], axis=1)
        left = pltpu.roll(line, 1, axis=1)[:, LANES : LANES + width]
        right = pltpu.roll(line, width + 2 * LANES - 1, axis=1)[:, LANES : LANES + width]
        neighbour = jnp.where(upward, left, right)
        out_ref[d] = (field - rate * (field - neighbour)).astype(jnp.bfloat16)


def advect(density, flags, courant, parts):
    nodes, cells = density.shape
    width = cells // parts
    wide = GROUP * width // LANES
    lines = cells // LANES
    return pl.pallas_call(
        advect_kernel,
        grid=(parts // GROUP,),
        out_shape=jax.ShapeDtypeStruct((parts, nodes, width), jnp.bfloat16),
        in_specs=[
            pl.BlockSpec(memory_space=pltpu.SMEM),
            pl.BlockSpec(memory_space=pltpu.SMEM),
            pl.BlockSpec((nodes, LANES), lambda i: (0, (i * wide + lines - 1) % lines)),
            pl.BlockSpec((nodes, GROUP * width), lambda i: (0, i)),
            pl.BlockSpec((nodes, LANES), lambda i: (0, ((i + 1) * wide) % lines)),
        ],
        out_specs=pl.BlockSpec((GROUP, nodes, width), lambda i: (i, 0, 0)),
        compiler_params=pltpu.CompilerParams(vmem_limit_bytes=24 << 20),
        cost_estimate=pl.CostEstimate(flops=4 * nodes * cells, bytes_accessed=4 * nodes * cells, transcendentals=0),
        name="advect",
    )(flags, courant, density, density, density)


def transform_kernel(s_ref, x_ref, c_ref):
    c_ref[...] = jnp.dot(s_ref[...], x_ref[...], preferred_element_type=jnp.float32).astype(jnp.bfloat16)


def transform(spectral, block, tile=512):
    size, width = spectral.shape[0], block.shape[1]
    return pl.pallas_call(
        transform_kernel,
        grid=(width // tile,),
        out_shape=jax.ShapeDtypeStruct((size, width), jnp.bfloat16),
        in_specs=[
            pl.BlockSpec(spectral.shape, lambda i: (0, 0)),
            pl.BlockSpec((block.shape[0], tile), lambda i: (0, i)),
        ],
        out_specs=pl.BlockSpec((size, tile), lambda i: (0, i)),
        compiler_params=pltpu.CompilerParams(vmem_limit_bytes=32 << 20),
        cost_estimate=pl.CostEstimate(
            flops=2 * size * block.shape[0] * width, bytes_accessed=6 * size * width, transcendentals=0
        ),
        name="transform",
    )(spectral, block)


def quadratic_kernel(u_hbm, c_ref, out_ref, u_ref, sems):
    size, tile = c_ref.shape
    count = size // BLOCK
    slots = out_ref.shape[0]
    pairs = fold_pairs(count)
    halves = BLOCK // LANES
    first = pl.program_id(0) == 0
    copies = [pltpu.make_async_copy(u_hbm.at[:, m], u_ref.at[m], sems.at[m]) for m in range(slots)]

    @pl.when(first)
    def _():
        for copy in copies:
            copy.start()

    factor = 1.0 / math.sqrt(size)
    for m in range(slots):
        pl.when(first)(copies[m].wait)
        flat = u_ref.at[m].reshape(u_ref.shape[1] * u_ref.shape[2], LANES)
        total = jnp.zeros((8, tile), jnp.float32)
        for i in range(count):
            panels = []
            for at, pair in enumerate(pairs):
                if pair[0] == i:
                    for half in range(halves):
                        panels.append(flat[pl.ds((at * halves + half) * BLOCK, BLOCK), :])
            strip = jnp.concatenate(panels, axis=1)
            image = jnp.dot(strip, c_ref[pl.ds(i * BLOCK, size - i * BLOCK), :], preferred_element_type=jnp.float32)
            term = image * c_ref[pl.ds(i * BLOCK, BLOCK), :].astype(jnp.float32)
            total = total + jnp.sum(term.reshape(BLOCK // 8, 8, tile), axis=0)
        out_ref[pl.ds(m, 1), :] = jnp.sum(total, axis=0, keepdims=True) * factor


def quadratic(gathered, coeffs, tile=512):
    size, width = coeffs.shape
    parts, slots, rows, lanes = gathered.shape
    return pl.pallas_call(
        quadratic_kernel,
        grid=(width // tile,),
        out_shape=jax.ShapeDtypeStruct((slots, width), jnp.float32),
        in_specs=[
            pl.BlockSpec(memory_space=pl.ANY),
            pl.BlockSpec((size, tile), lambda i: (0, i)),
        ],
        out_specs=pl.BlockSpec((slots, tile), lambda i: (0, i)),
        scratch_shapes=[
            pltpu.VMEM((slots, parts, rows, lanes), jnp.bfloat16),
            pltpu.SemaphoreType.DMA((slots,)),
        ],
        compiler_params=pltpu.CompilerParams(vmem_limit_bytes=40 << 20),
        cost_estimate=pl.CostEstimate(
            flops=2 * slots * parts * rows * lanes * width, bytes_accessed=6 * size * width, transcendentals=0
        ),
        name="quadratic",
    )(gathered, coeffs)


def local(parts, density, flags, courant, spectral, tensor, owner):
    folded = fold(tensor)
    pieces = lax.all_to_all(folded.reshape(parts, -1, LANES), "dev", split_axis=0, concat_axis=0, tiled=True)
    chosen = jnp.stack([lax.dynamic_index_in_dim(pieces, owner[m], 0, keepdims=False) for m in range(owner.shape[0])])
    gathered = lax.all_gather(chosen, "dev", axis=0)
    moved = advect(density, flags, courant, parts)
    arrived = lax.all_to_all(moved, "dev", split_axis=0, concat_axis=0, tiled=True)
    coeffs = transform(spectral, arrived.reshape(-1, arrived.shape[2]))
    return (coeffs, quadratic(gathered, coeffs))


def solution(mesh):
    in_specs = (P("dev", None), P("dev"), P("dev"), P(), P("dev", None, None), P())
    out_specs = (P(None, "dev"), P(None, "dev"))

    def step(*args):
        return local(mesh.shape["dev"], *args)

    return jax.shard_map(step, mesh=mesh, in_specs=in_specs, out_specs=out_specs, check_vma=False)
```

```python
import functools
import math

import jax
import jax.numpy as jnp
from jax import lax
from jax.experimental import pallas as pl
from jax.experimental.pallas import tpu as pltpu
from jax.sharding import PartitionSpec as P

BLOCK = 256
LANES = 128
GROUP = 8
SUBLANES = 8
LIMIT = 60 << 20


def fold_kernel(t_hbm, u_ref, e_ref, t_ref, sems):
    count = t_ref.shape[0] // BLOCK
    halves = BLOCK // LANES
    copies = []
    for i in range(count):
        rows = pl.ds(i * BLOCK, BLOCK)
        copies.append(pltpu.make_async_copy(t_hbm.at[0, rows, :], t_ref.at[rows, :], sems.at[i]))
        copies[i].start()

    def load(i, j):
        return t_ref[pl.ds(i * BLOCK, BLOCK), pl.ds(j * BLOCK, BLOCK)].astype(jnp.float32)

    def store(at, block):
        block = block.astype(jnp.bfloat16)
        for half in range(halves):
            u_ref[pl.ds((at * halves + half) * BLOCK, BLOCK), :] = block[:, half * LANES : (half + 1) * LANES]

    row = lax.broadcasted_iota(jnp.int32, (BLOCK, BLOCK), 0)
    col = lax.broadcasted_iota(jnp.int32, (BLOCK, BLOCK), 1)
    above = above_pairs(count)
    e_ref[...] = jnp.zeros_like(e_ref)
    for j in range(count):
        copies[j].wait()
        for i in range(j):
            store(above.index((i, j)), load(i, j) + load(j, i).T)
        if j % 2 == 1:
            upper, lower = load(j - 1, j - 1), load(j, j)
            packed = jnp.where(row < col, upper + upper.T, jnp.where(row == col, upper, lower + lower.T))
            store(len(above) + j // 2, packed)
            line = jnp.sum(jnp.where(row == col, lower, 0.0), axis=0, keepdims=True).astype(jnp.bfloat16)
            for half in range(halves):
                e_ref[pl.ds(j // 2 * halves + half, 1), :] = line[:, half * LANES : (half + 1) * LANES]


def above_pairs(count):
    return [(i, j) for j in range(count) for i in range(j)]


def fold(tensor):
    size = tensor.shape[1]
    count = size // BLOCK
    rows = (len(above_pairs(count)) + count // 2) * BLOCK * (BLOCK // LANES)
    return pl.pallas_call(
        fold_kernel,
        out_shape=[
            jax.ShapeDtypeStruct((rows, LANES), jnp.bfloat16),
            jax.ShapeDtypeStruct((SUBLANES, LANES), jnp.bfloat16),
        ],
        in_specs=[pl.BlockSpec(memory_space=pltpu.HBM)],
        out_specs=[pl.BlockSpec(memory_space=pltpu.VMEM)] * 2,
        scratch_shapes=[pltpu.VMEM((size, size), jnp.bfloat16), pltpu.SemaphoreType.DMA((count,))],
        compiler_params=pltpu.CompilerParams(vmem_limit_bytes=LIMIT),
        cost_estimate=pl.CostEstimate(flops=2 * size * size, bytes_accessed=3 * size * size, transcendentals=0),
        name="fold",
    )(tensor)


def advect_kernel(flags_ref, courant_ref, before_ref, here_ref, after_ref, out_ref):
    nodes = here_ref.shape[0]
    width = here_ref.shape[1] // out_ref.shape[0]
    row = lax.broadcasted_iota(jnp.int32, (nodes, 1), 0)
    flag = jnp.zeros((nodes, 1), jnp.int32)
    rate = jnp.zeros((nodes, 1), jnp.float32)
    for r in range(nodes):
        flag = jnp.where(row == r, flags_ref[r], flag)
        rate = jnp.where(row == r, courant_ref[r], rate)
    upward = jnp.broadcast_to(flag, (nodes, width)) == 1
    for d in range(out_ref.shape[0]):
        start, stop = d * width, (d + 1) * width
        last = d == out_ref.shape[0] - 1
        before = before_ref[...] if d == 0 else here_ref[:, start - LANES : start]
        after = after_ref[...] if last else here_ref[:, stop : stop + LANES]
        field = here_ref[:, start:stop].astype(jnp.float32)
        line = jnp.concatenate([before.astype(jnp.float32), field, after.astype(jnp.float32)], axis=1)
        left = pltpu.roll(line, 1, axis=1)[:, LANES : LANES + width]
        right = pltpu.roll(line, width + 2 * LANES - 1, axis=1)[:, LANES : LANES + width]
        neighbour = jnp.where(upward, left, right)
        moved = (field - rate * (field - neighbour)).astype(jnp.bfloat16)
        for t in range(width // LANES):
            out_ref[d, t * nodes : (t + 1) * nodes, :] = moved[:, t * LANES : (t + 1) * LANES]


def advect(density, flags, courant, parts, spare):
    nodes, cells = density.shape
    width = cells // parts
    wide = GROUP * width // LANES
    lines = cells // LANES
    rows = nodes * width // LANES
    return pl.pallas_call(
        advect_kernel,
        grid=(parts // GROUP,),
        out_shape=jax.ShapeDtypeStruct((parts, rows + spare, LANES), jnp.bfloat16),
        in_specs=[
            pl.BlockSpec(memory_space=pltpu.SMEM),
            pl.BlockSpec(memory_space=pltpu.SMEM),
            pl.BlockSpec((nodes, LANES), lambda i: (0, (i * wide + lines - 1) % lines)),
            pl.BlockSpec((nodes, GROUP * width), lambda i: (0, i)),
            pl.BlockSpec((nodes, LANES), lambda i: (0, ((i + 1) * wide) % lines)),
        ],
        out_specs=pl.BlockSpec((GROUP, rows, LANES), lambda i: (i, 0, 0)),
        compiler_params=pltpu.CompilerParams(vmem_limit_bytes=LIMIT),
        cost_estimate=pl.CostEstimate(flops=4 * nodes * cells, bytes_accessed=4 * nodes * cells, transcendentals=0),
        name="advect",
    )(flags, courant, density, density, density)


def pick_kernel(owner_ref, pieces_ref, extra_ref, _, out_hbm, spread_ref, sems):
    half = owner_ref.shape[0] // 2
    batch, rows = spread_ref.shape[0], spread_ref.shape[1]
    first = out_hbm.shape[1] - rows
    chosen = [pieces_ref[owner_ref[m]] for m in range(2 * half)]
    extra = extra_ref[...]
    for d in range(batch):
        core, z, y = d % 2, d // 2 % 4, d // 8 % 4
        quarter = (y if core else z) * SUBLANES
        for s in range(half):
            part = chosen[core * half + s][quarter : quarter + SUBLANES, :]
            spread_ref[d, s * SUBLANES : (s + 1) * SUBLANES, :] = part
        spread_ref[d, half * SUBLANES : (half + 1) * SUBLANES, :] = extra
    writes = []
    for b in range(out_hbm.shape[0] // batch):
        target = out_hbm.at[pl.ds(b * batch, batch), pl.ds(first, rows), :]
        writes.append(pltpu.make_async_copy(spread_ref, target, sems.at[b]))
    for write in writes:
        write.start()
    for write in writes:
        write.wait()


def pick(owner, pieces, extra, moved, spare, batch=32):
    parts = pieces.shape[0]
    return pl.pallas_call(
        pick_kernel,
        out_shape=jax.ShapeDtypeStruct(moved.shape, moved.dtype),
        in_specs=[
            pl.BlockSpec(memory_space=pltpu.SMEM),
            pl.BlockSpec(memory_space=pltpu.VMEM),
            pl.BlockSpec(memory_space=pltpu.VMEM),
            pl.BlockSpec(memory_space=pltpu.HBM),
        ],
        out_specs=pl.BlockSpec(memory_space=pltpu.HBM),
        scratch_shapes=[
            pltpu.VMEM((batch, spare, LANES), jnp.bfloat16),
            pltpu.SemaphoreType.DMA((parts // batch,)),
        ],
        input_output_aliases={3: 0},
        compiler_params=pltpu.CompilerParams(vmem_limit_bytes=32 << 20),
        cost_estimate=pl.CostEstimate(flops=0, bytes_accessed=parts * spare * LANES * 2, transcendentals=0),
        name="pick",
    )(owner, pieces, extra, moved)


def unpack_kernel(owner_ref, arrived, near_ref, e_ref, sems):
    slots = e_ref.shape[0]
    end = arrived.shape[1] - SUBLANES
    first = end - near_ref.shape[1]
    copies = [pltpu.make_async_copy(arrived.at[:, pl.ds(first, end - first), :], near_ref, sems.at[slots])]
    for m in range(slots):
        last = arrived.at[owner_ref[m], pl.ds(end, SUBLANES), :]
        copies.append(pltpu.make_async_copy(last, e_ref.at[m], sems.at[m]))
    for copy in copies:
        copy.start()
    for copy in copies:
        copy.wait()


def unpack(owner, arrived, rows):
    slots = owner.shape[0]
    parts = arrived.shape[0]
    return pl.pallas_call(
        unpack_kernel,
        out_shape=[
            jax.ShapeDtypeStruct((parts, rows, LANES), jnp.bfloat16),
            jax.ShapeDtypeStruct((slots, SUBLANES, LANES), jnp.bfloat16),
        ],
        in_specs=[pl.BlockSpec(memory_space=pltpu.SMEM), pl.BlockSpec(memory_space=pl.ANY)],
        out_specs=[pl.BlockSpec(memory_space=pltpu.VMEM)] * 2,
        scratch_shapes=[pltpu.SemaphoreType.DMA((slots + 1,))],
        compiler_params=pltpu.CompilerParams(vmem_limit_bytes=LIMIT),
        cost_estimate=pl.CostEstimate(flops=0, bytes_accessed=4 * parts * rows * LANES, transcendentals=0),
        name="unpack",
    )(owner, arrived)


def transform_kernel(s_ref, x_ref, c_ref):
    parts, rows, lanes = x_ref.shape
    nodes = s_ref.shape[1] // parts
    columns = [x_ref[:, t : t + nodes, :].reshape(parts * nodes, lanes) for t in range(0, rows, nodes)]
    block = jnp.concatenate(columns, axis=1)
    c_ref[...] = jnp.dot(s_ref[...], block, preferred_element_type=jnp.float32).astype(jnp.bfloat16)


def transform(spectral, arrived, width, tile=512):
    size = spectral.shape[0]
    parts = arrived.shape[0]
    nodes = spectral.shape[1] // parts
    return pl.pallas_call(
        transform_kernel,
        grid=(width // tile,),
        out_shape=jax.ShapeDtypeStruct((size, width), jnp.bfloat16),
        in_specs=[
            pl.BlockSpec(spectral.shape, lambda i: (0, 0)),
            pl.BlockSpec((parts, nodes * tile // LANES, LANES), lambda i: (0, i, 0)),
        ],
        out_specs=pl.BlockSpec((size, tile), lambda i: (0, i)),
        compiler_params=pltpu.CompilerParams(vmem_limit_bytes=LIMIT),
        cost_estimate=pl.CostEstimate(
            flops=2 * size * size * width, bytes_accessed=6 * size * width, transcendentals=0
        ),
        name="transform",
    )(spectral, arrived)


def quadratic_kernel(mine, q0, q1, q2, q3, e_ref, c_ref, *refs):
    before_ref = None if mine else refs[0]
    out_ref, u_ref, sems = refs[-3:]
    size, tile = c_ref.shape
    count = size // BLOCK
    half = u_ref.shape[0]
    halves = BLOCK // LANES
    above = above_pairs(count)
    first = pl.program_id(0) == 0
    here = lax.axis_index("dev")
    core = here % 2 if mine else 1 - here % 2
    start = jnp.where(core == 0, here // 2, here // 8)
    copies = []
    for s in range(half):
        for k, source in enumerate((q0, q1, q2, q3)):
            quarter = (start + 4 - k) % 4
            rows = source.at[:, pl.ds(s * SUBLANES, SUBLANES), :]
            copies.append(pltpu.make_async_copy(rows, u_ref.at[s, :, quarter], sems.at[s, k]))

    def panel(flat, at):
        parts = [flat[pl.ds((at * halves + part) * BLOCK, BLOCK), :] for part in range(halves)]
        return jnp.concatenate(parts, axis=1)

    @pl.when(first)
    def _():
        for copy in copies:
            copy.start()

    if not mine:
        out_ref[...] = before_ref[...]
    factor = 1.0 / math.sqrt(size)
    row = lax.broadcasted_iota(jnp.int32, (BLOCK, BLOCK), 0)
    col = lax.broadcasted_iota(jnp.int32, (BLOCK, BLOCK), 1)
    for s in range(half):

        @pl.when(first)
        def _():
            for copy in copies[s * 4 : s * 4 + 4]:
                copy.wait()

        flat = u_ref.at[s].reshape(math.prod(u_ref.shape[1:4]), LANES)
        total = jnp.zeros((SUBLANES, tile), jnp.float32)
        for i in range(count):
            packed = panel(flat, len(above) + i // 2).astype(jnp.float32)
            if i % 2 == 0:
                diagonal = jnp.where(row <= col, packed, 0.0)
            else:
                lines = [e_ref[core * half + s, pl.ds(i // 2 * halves + part, 1), :] for part in range(halves)]
                line = jnp.concatenate(lines, axis=1).astype(jnp.float32)
                diagonal = jnp.where(row > col, packed, jnp.where(row == col, line, 0.0))
            panels = [diagonal.astype(jnp.bfloat16)]
            panels += [panel(flat, above.index((i, j))) for j in range(i + 1, count)]
            strip = jnp.concatenate(panels, axis=1)
            image = jnp.dot(strip, c_ref[pl.ds(i * BLOCK, size - i * BLOCK), :], preferred_element_type=jnp.float32)
            term = image * c_ref[pl.ds(i * BLOCK, BLOCK), :].astype(jnp.float32)
            total = total + jnp.sum(term.reshape(BLOCK // SUBLANES, SUBLANES, tile), axis=0)
        out_ref[pl.ds(core * half + s, 1), :] = jnp.sum(total, axis=0, keepdims=True) * factor


def quadratic(quarters, diagonals, coeffs, before, tile=512):
    size, width = coeffs.shape
    parts = quarters[0].shape[0]
    slots = diagonals.shape[0]
    half = slots // 2
    out_spec = pl.BlockSpec((slots, tile), lambda i: (0, i))
    args = [*quarters, diagonals, coeffs]
    in_specs = [
        *[pl.BlockSpec(memory_space=pl.ANY)] * 4,
        pl.BlockSpec(diagonals.shape, lambda i: (0, 0, 0)),
        pl.BlockSpec((size, tile), lambda i: (0, i)),
    ]
    if before is not None:
        args.append(before)
        in_specs.append(out_spec)
    return pl.pallas_call(
        functools.partial(quadratic_kernel, before is None),
        grid=(width // tile,),
        out_shape=jax.ShapeDtypeStruct((slots, width), jnp.float32),
        in_specs=in_specs,
        out_specs=out_spec,
        scratch_shapes=[
            pltpu.VMEM((half, parts, 4, SUBLANES, LANES), jnp.bfloat16),
            pltpu.SemaphoreType.DMA((half, 4)),
        ],
        compiler_params=pltpu.CompilerParams(vmem_limit_bytes=48 << 20),
        cost_estimate=pl.CostEstimate(
            flops=half * size * size * width * 5 // 4, bytes_accessed=2 * size * width, transcendentals=0
        ),
        name="quadratic",
    )(*args)


def exchange(x):
    return lax.all_to_all(x, "dev", split_axis=0, concat_axis=0, tiled=True)


def shift(parts, k):
    pairs = []
    for d in range(parts):
        step = 8 if d % 2 else 2
        at = d // step % 4
        pairs.append((d, d + ((at + k) % 4 - at) * step))
    return pairs


def local(parts, density, flags, courant, spectral, tensor, owner):
    half = owner.shape[0] // 2
    width = density.shape[1] // parts
    spare = (half + 1) * SUBLANES
    folded, extra = fold(tensor)
    pieces = exchange(folded.reshape(parts, -1, LANES))
    moved = advect(density, flags, courant, parts, spare)
    arrived = exchange(pick(owner, pieces, extra, moved, spare))
    first, diagonals = unpack(owner, arrived, half * SUBLANES)
    near = [first] + [lax.ppermute(first, "dev", shift(parts, k)) for k in (1, 2, 3)]
    coeffs = transform(spectral, arrived, width)
    *near, coeffs = lax.optimization_barrier((*near, coeffs))
    far = [lax.ppermute(x, "dev", [(d, d ^ 1) for d in range(parts)]) for x in near]
    own = quadratic(near, diagonals, coeffs, None)
    return (coeffs, quadratic(far, diagonals, coeffs, own))


def solution(mesh):
    in_specs = (P("dev", None), P("dev"), P("dev"), P(), P("dev", None, None), P())
    out_specs = (P(None, "dev"), P(None, "dev"))

    def step(*args):
        return local(mesh.shape["dev"], *args)

    return jax.shard_map(step, mesh=mesh, in_specs=in_specs, out_specs=out_specs, check_vma=False)
```

```python
import functools
import math

import jax
import jax.numpy as jnp
from jax import lax
from jax.experimental import pallas as pl
from jax.experimental.pallas import tpu as pltpu
from jax.sharding import PartitionSpec as P

BLOCK = 256
LANES = 128
GROUP = 8
SUBLANES = 8
LIMIT = 24 << 20
HIGH = 58 << 20


def fold_kernel(t_hbm, u_ref, e_ref, t_ref, sems):
    count = t_ref.shape[0] // BLOCK
    halves = BLOCK // LANES
    copies = []
    for i in range(count):
        rows = pl.ds(i * BLOCK, BLOCK)
        copies.append(pltpu.make_async_copy(t_hbm.at[0, rows, :], t_ref.at[rows, :], sems.at[i]))
        copies[i].start()

    def load(i, j):
        return t_ref[pl.ds(i * BLOCK, BLOCK), pl.ds(j * BLOCK, BLOCK)].astype(jnp.float32)

    def store(at, block):
        block = block.astype(jnp.bfloat16)
        for half in range(halves):
            quarter, run = divmod(at * halves + half, 4)
            lines = block[:, half * LANES : (half + 1) * LANES].reshape(run_length, SUBLANES, LANES)
            u_ref[pl.ds(run * run_length, run_length), pl.ds(quarter * SUBLANES, SUBLANES), :] = lines

    run_length = BLOCK // SUBLANES
    row = lax.broadcasted_iota(jnp.int32, (BLOCK, BLOCK), 0)
    col = lax.broadcasted_iota(jnp.int32, (BLOCK, BLOCK), 1)
    above = above_pairs(count)
    e_ref[...] = jnp.zeros_like(e_ref)
    for j in range(count):
        copies[j].wait()
        for i in range(j):
            store(above.index((i, j)), load(i, j) + load(j, i).T)
        if j % 2 == 1:
            upper, lower = load(j - 1, j - 1), load(j, j)
            packed = jnp.where(row < col, upper + upper.T, jnp.where(row == col, upper, lower + lower.T))
            store(len(above) + j // 2, packed)
            line = jnp.sum(jnp.where(row == col, lower, 0.0), axis=0, keepdims=True).astype(jnp.bfloat16)
            for half in range(halves):
                e_ref[pl.ds(j // 2 * halves + half, 1), :] = line[:, half * LANES : (half + 1) * LANES]


def above_pairs(count):
    return [(i, j) for j in range(count) for i in range(j)]


def fold(tensor):
    size = tensor.shape[1]
    count = size // BLOCK
    rows = (len(above_pairs(count)) + count // 2) * BLOCK * (BLOCK // LANES)
    parts = rows // (4 * SUBLANES)
    return pl.pallas_call(
        fold_kernel,
        out_shape=[
            jax.ShapeDtypeStruct((parts, 4 * SUBLANES, LANES), jnp.bfloat16),
            jax.ShapeDtypeStruct((SUBLANES, LANES), jnp.bfloat16),
        ],
        in_specs=[pl.BlockSpec(memory_space=pltpu.HBM)],
        out_specs=[pl.BlockSpec(memory_space=pltpu.VMEM)] * 2,
        scratch_shapes=[pltpu.VMEM((size, size), jnp.bfloat16), pltpu.SemaphoreType.DMA((count,))],
        compiler_params=pltpu.CompilerParams(vmem_limit_bytes=HIGH),
        cost_estimate=pl.CostEstimate(flops=2 * size * size, bytes_accessed=3 * size * size, transcendentals=0),
        name="fold",
    )(tensor)


def advect_kernel(flags_ref, courant_ref, before_ref, here_ref, after_ref, out_ref):
    nodes = here_ref.shape[0]
    width = here_ref.shape[1] // out_ref.shape[0]
    row = lax.broadcasted_iota(jnp.int32, (nodes, 1), 0)
    flag = jnp.zeros((nodes, 1), jnp.int32)
    rate = jnp.zeros((nodes, 1), jnp.float32)
    for r in range(nodes):
        flag = jnp.where(row == r, flags_ref[r], flag)
        rate = jnp.where(row == r, courant_ref[r], rate)
    upward = jnp.broadcast_to(flag, (nodes, width)) == 1
    for d in range(out_ref.shape[0]):
        start, stop = d * width, (d + 1) * width
        last = d == out_ref.shape[0] - 1
        before = before_ref[...] if d == 0 else here_ref[:, start - LANES : start]
        after = after_ref[...] if last else here_ref[:, stop : stop + LANES]
        field = here_ref[:, start:stop].astype(jnp.float32)
        line = jnp.concatenate([before.astype(jnp.float32), field, after.astype(jnp.float32)], axis=1)
        left = pltpu.roll(line, 1, axis=1)[:, LANES : LANES + width]
        right = pltpu.roll(line, width + 2 * LANES - 1, axis=1)[:, LANES : LANES + width]
        neighbour = jnp.where(upward, left, right)
        moved = (field - rate * (field - neighbour)).astype(jnp.bfloat16)
        for t in range(width // LANES):
            out_ref[d, t * nodes : (t + 1) * nodes, :] = moved[:, t * LANES : (t + 1) * LANES]


def advect(density, flags, courant, parts, spare):
    nodes, cells = density.shape
    width = cells // parts
    wide = GROUP * width // LANES
    lines = cells // LANES
    rows = nodes * width // LANES
    return pl.pallas_call(
        advect_kernel,
        grid=(parts // GROUP,),
        out_shape=jax.ShapeDtypeStruct((parts, rows + spare, LANES), jnp.bfloat16),
        in_specs=[
            pl.BlockSpec(memory_space=pltpu.SMEM),
            pl.BlockSpec(memory_space=pltpu.SMEM),
            pl.BlockSpec((nodes, LANES), lambda i: (0, (i * wide + lines - 1) % lines)),
            pl.BlockSpec((nodes, GROUP * width), lambda i: (0, i)),
            pl.BlockSpec((nodes, LANES), lambda i: (0, ((i + 1) * wide) % lines)),
        ],
        out_specs=pl.BlockSpec((GROUP, rows, LANES), lambda i: (i, 0, 0)),
        compiler_params=pltpu.CompilerParams(vmem_limit_bytes=HIGH),
        cost_estimate=pl.CostEstimate(flops=4 * nodes * cells, bytes_accessed=4 * nodes * cells, transcendentals=0),
        name="advect",
    )(flags, courant, density, density, density)


def pick_kernel(owner_ref, pieces_ref, extra_ref, _, out_hbm, spread_ref, sems):
    half = owner_ref.shape[0] // 2
    batch, rows = spread_ref.shape[0], spread_ref.shape[1]
    first = out_hbm.shape[1] - rows
    chosen = [pieces_ref[owner_ref[m]] for m in range(2 * half)]
    extra = extra_ref[...]
    for d in range(batch):
        core, z, y = d % 2, d // 2 % 4, d // 8 % 4
        quarter = (y if core else z) * SUBLANES
        for s in range(half):
            part = chosen[core * half + s][quarter : quarter + SUBLANES, :]
            spread_ref[d, s * SUBLANES : (s + 1) * SUBLANES, :] = part
        spread_ref[d, half * SUBLANES : (half + 1) * SUBLANES, :] = extra
    writes = []
    for b in range(out_hbm.shape[0] // batch):
        target = out_hbm.at[pl.ds(b * batch, batch), pl.ds(first, rows), :]
        writes.append(pltpu.make_async_copy(spread_ref, target, sems.at[b]))
    for write in writes:
        write.start()
    for write in writes:
        write.wait()


def pick(owner, pieces, extra, moved, spare, batch=32):
    parts = pieces.shape[0]
    return pl.pallas_call(
        pick_kernel,
        out_shape=jax.ShapeDtypeStruct(moved.shape, moved.dtype),
        in_specs=[
            pl.BlockSpec(memory_space=pltpu.SMEM),
            pl.BlockSpec(memory_space=pltpu.VMEM),
            pl.BlockSpec(memory_space=pltpu.VMEM),
            pl.BlockSpec(memory_space=pl.ANY),
        ],
        out_specs=pl.BlockSpec(memory_space=pl.ANY),
        scratch_shapes=[
            pltpu.VMEM((batch, spare, LANES), jnp.bfloat16),
            pltpu.SemaphoreType.DMA((parts // batch,)),
        ],
        input_output_aliases={3: 0},
        compiler_params=pltpu.CompilerParams(vmem_limit_bytes=HIGH),
        cost_estimate=pl.CostEstimate(flops=0, bytes_accessed=parts * spare * LANES * 2, transcendentals=0),
        name="pick",
    )(owner, pieces, extra, moved)


def unpack_kernel(owner_ref, arrived, near_ref, e_ref):
    end = arrived.shape[1] - SUBLANES
    near_ref[...] = arrived[:, end - near_ref.shape[1] : end, :]
    for m in range(e_ref.shape[0]):
        e_ref[m] = arrived[owner_ref[m], end:, :]


def unpack(owner, arrived, rows):
    slots = owner.shape[0]
    parts = arrived.shape[0]
    return pl.pallas_call(
        unpack_kernel,
        out_shape=[
            jax.ShapeDtypeStruct((parts, rows, LANES), jnp.bfloat16),
            jax.ShapeDtypeStruct((slots, SUBLANES, LANES), jnp.bfloat16),
        ],
        in_specs=[pl.BlockSpec(memory_space=pltpu.SMEM), pl.BlockSpec(memory_space=pltpu.VMEM)],
        out_specs=[pl.BlockSpec(memory_space=pltpu.VMEM)] * 2,
        compiler_params=pltpu.CompilerParams(vmem_limit_bytes=LIMIT),
        cost_estimate=pl.CostEstimate(flops=0, bytes_accessed=4 * parts * rows * LANES, transcendentals=0),
        name="unpack",
    )(owner, arrived)


def transform_kernel(tile, s_ref, x_ref, c_hbm, c_ref, sems):
    parts = x_ref.shape[0]
    nodes = s_ref.shape[1] // parts
    writes = []
    for n in range(c_ref.shape[1] // tile):
        lines = range(n * tile // LANES * nodes, (n + 1) * tile // LANES * nodes, nodes)
        columns = [x_ref[:, t : t + nodes, :].reshape(parts * nodes, LANES) for t in lines]
        block = jnp.concatenate(columns, axis=1)
        cells = pl.ds(n * tile, tile)
        c_ref[:, cells] = jnp.dot(s_ref[...], block, preferred_element_type=jnp.float32).astype(jnp.bfloat16)
        writes.append(pltpu.make_async_copy(c_ref.at[:, cells], c_hbm.at[:, cells], sems.at[n]))
        writes[n].start()
    for write in writes:
        write.wait()


def transform(spectral, arrived, width, tile=512):
    size = spectral.shape[0]
    return pl.pallas_call(
        functools.partial(transform_kernel, tile),
        out_shape=[jax.ShapeDtypeStruct((size, width), jnp.bfloat16)] * 2,
        in_specs=[pl.BlockSpec(memory_space=pltpu.VMEM)] * 2,
        out_specs=[pl.BlockSpec(memory_space=pl.ANY), pl.BlockSpec(memory_space=pltpu.VMEM)],
        scratch_shapes=[pltpu.SemaphoreType.DMA((width // tile,))],
        compiler_params=pltpu.CompilerParams(vmem_limit_bytes=LIMIT),
        cost_estimate=pl.CostEstimate(
            flops=2 * size * size * width, bytes_accessed=6 * size * width, transcendentals=0
        ),
        name="transform",
    )(spectral, arrived)


def quadratic_kernel(pairs, tile, e_ref, c_ref, *refs):
    sources, out_ref = refs[: len(pairs)], refs[-1]
    size, width = c_ref.shape
    halves = BLOCK // LANES
    run = BLOCK // SUBLANES
    half = e_ref.shape[0] // 2
    above = above_pairs(size // BLOCK)
    row = lax.broadcasted_iota(jnp.int32, (BLOCK, BLOCK), 0)
    col = lax.broadcasted_iota(jnp.int32, (BLOCK, BLOCK), 1)
    factor = 1.0 / math.sqrt(size)
    here = lax.axis_index("dev")
    if len(refs) > len(pairs) + 1:
        out_ref[...] = refs[len(pairs)][...]
    else:
        out_ref[...] = jnp.zeros_like(out_ref)

    def add(core, both, i, j):
        left = pl.ds(pl.multiple_of(i * BLOCK, BLOCK), BLOCK)
        right = pl.ds(pl.multiple_of(j * BLOCK, BLOCK), BLOCK)
        for first in range(0, width, tile):
            cells = slice(first, first + tile)
            image = jnp.dot(both, c_ref[right, cells], preferred_element_type=jnp.float32)
            weight = c_ref[left, cells].astype(jnp.float32)
            for s in range(half):
                term = image[s * BLOCK : (s + 1) * BLOCK] * weight
                line = jnp.sum(jnp.sum(term.reshape(run, SUBLANES, tile), axis=0), axis=0, keepdims=True)
                out_ref[pl.ds(core * half + s, 1), cells] += line * factor

    for source, (mine, k) in zip(sources, pairs):
        core = here % 2 if mine else 1 - here % 2
        quarter = (jnp.where(core == 0, here // 2, here // 8) + 4 - k) % 4

        def block(s, b, source=source):
            panels = []
            for part in range(halves):
                first = (b * halves + part) * run
                lines = source[first : first + run, s * SUBLANES : (s + 1) * SUBLANES, :]
                panels.append(lines.reshape(BLOCK, LANES))
            return jnp.concatenate(panels, axis=1)

        def choose(table, quarter=quarter):
            value = table[0]
            for at in range(1, len(table)):
                value = jnp.where(quarter == at, table[at], value)
            return value

        full = len(above) // 2

        @pl.when(quarter < full)
        def _(core=core, block=block, choose=choose):
            for b in range(2):
                i, j = (choose([above[2 * q + b][side] for q in range(full)]) for side in range(2))
                add(core, jnp.concatenate([block(s, b) for s in range(half)], axis=0), i, j)

        @pl.when(quarter == full)
        def _(core=core, block=block):
            for b in range(2):
                packed = [block(s, b).astype(jnp.float32) for s in range(half)]
                upper = [jnp.where(row <= col, x, 0.0) for x in packed]
                lower = []
                for s, x in enumerate(packed):
                    values = [e_ref[core * half + s, pl.ds(b * halves + part, 1), :] for part in range(halves)]
                    line = jnp.concatenate(values, axis=1).astype(jnp.float32)
                    lower.append(jnp.where(row > col, x, jnp.where(row == col, line, 0.0)))
                add(core, jnp.concatenate(upper, axis=0).astype(jnp.bfloat16), 2 * b, 2 * b)
                add(core, jnp.concatenate(lower, axis=0).astype(jnp.bfloat16), 2 * b + 1, 2 * b + 1)


def quadratic(pairs, sources, diagonals, coeffs, before=None, tile=512):
    size, width = coeffs.shape
    slots = diagonals.shape[0]
    args = [diagonals, coeffs, *sources] + ([] if before is None else [before])
    return pl.pallas_call(
        functools.partial(quadratic_kernel, pairs, tile),
        out_shape=jax.ShapeDtypeStruct((slots, width), jnp.float32),
        in_specs=[pl.BlockSpec(memory_space=pltpu.VMEM)] * len(args),
        out_specs=pl.BlockSpec(memory_space=pltpu.VMEM),
        compiler_params=pltpu.CompilerParams(vmem_limit_bytes=LIMIT),
        cost_estimate=pl.CostEstimate(
            flops=len(pairs) * size * size * width * 5 // 16, bytes_accessed=2 * size * width, transcendentals=0
        ),
        name="quadratic",
    )(*args)


def exchange(x):
    return lax.all_to_all(x, "dev", split_axis=0, concat_axis=0, tiled=True)


def shift(parts, k):
    pairs = []
    for d in range(parts):
        step = 8 if d % 2 else 2
        at = d // step % 4
        pairs.append((d, d + ((at + k) % 4 - at) * step))
    return pairs


def local(parts, density, flags, courant, spectral, tensor, owner):
    half = owner.shape[0] // 2
    width = density.shape[1] // parts
    spare = (half + 1) * SUBLANES
    folded, extra = fold(tensor)
    pieces = exchange(folded)
    moved = advect(density, flags, courant, parts, spare)
    arrived = exchange(pick(owner, pieces, extra, moved, spare))
    first, diagonals = unpack(owner, arrived, half * SUBLANES)
    pair = [(d, d ^ 1) for d in range(parts)]
    hops = (1, 2, 3)
    near = [lax.ppermute(first, "dev", shift(parts, k)) for k in hops]
    other = lax.ppermute(first, "dev", pair)
    result, coeffs = transform(spectral, arrived, width)
    begun = quadratic([(True, 0), (False, 0)], [first, other], diagonals, coeffs)
    *near, begun = lax.optimization_barrier((*near, begun))
    far = [lax.ppermute(x, "dev", pair) for x in near]
    own = quadratic([(True, k) for k in hops], near, diagonals, coeffs, begun)
    return (result, quadratic([(False, k) for k in hops], far, diagonals, coeffs, own))


def solution(mesh):
    in_specs = (P("dev", None), P("dev"), P("dev"), P(), P("dev", None, None), P())
    out_specs = (P(None, "dev"), P(None, "dev"))

    def step(*args):
        return local(mesh.shape["dev"], *args)

    return jax.shard_map(step, mesh=mesh, in_specs=in_specs, out_specs=out_specs, check_vma=False)
```

```python
import functools
import math

import jax
import jax.numpy as jnp
from jax import lax
from jax.experimental import pallas as pl
from jax.experimental.pallas import tpu as pltpu
from jax.sharding import PartitionSpec as P

BLOCK = 256
LANES = 128
GROUP = 8
SUBLANES = 8
LIMIT = 24 << 20
HIGH = 58 << 20


def fold_kernel(t_hbm, u_ref, e_ref, t_ref, sems):
    count = t_ref.shape[0] // BLOCK
    halves = BLOCK // LANES
    copies = []
    for i in range(count):
        rows = pl.ds(i * BLOCK, BLOCK)
        copies.append(pltpu.make_async_copy(t_hbm.at[0, rows, :], t_ref.at[rows, :], sems.at[i]))
        copies[i].start()

    def load(i, j):
        return t_ref[pl.ds(i * BLOCK, BLOCK), pl.ds(j * BLOCK, BLOCK)].astype(jnp.float32)

    def store(at, block):
        block = block.astype(jnp.bfloat16)
        for half in range(halves):
            quarter, run = divmod(at * halves + half, 4)
            lines = block[:, half * LANES : (half + 1) * LANES].reshape(run_length, SUBLANES, LANES)
            u_ref[pl.ds(run * run_length, run_length), pl.ds(quarter * SUBLANES, SUBLANES), :] = lines

    run_length = BLOCK // SUBLANES
    row = lax.broadcasted_iota(jnp.int32, (BLOCK, BLOCK), 0)
    col = lax.broadcasted_iota(jnp.int32, (BLOCK, BLOCK), 1)
    above = above_pairs(count)
    e_ref[...] = jnp.zeros_like(e_ref)
    for j in range(count):
        copies[j].wait()
        for i in range(j):
            store(above.index((i, j)), load(i, j) + load(j, i).T)
        if j % 2 == 1:
            upper, lower = load(j - 1, j - 1), load(j, j)
            packed = jnp.where(row < col, upper + upper.T, jnp.where(row == col, upper, lower + lower.T))
            store(len(above) + j // 2, packed)
            line = jnp.sum(jnp.where(row == col, lower, 0.0), axis=0, keepdims=True).astype(jnp.bfloat16)
            for half in range(halves):
                e_ref[pl.ds(j // 2 * halves + half, 1), :] = line[:, half * LANES : (half + 1) * LANES]


def above_pairs(count):
    return [(i, j) for j in range(count) for i in range(j)]


def fold(tensor):
    size = tensor.shape[1]
    count = size // BLOCK
    rows = (len(above_pairs(count)) + count // 2) * BLOCK * (BLOCK // LANES)
    parts = rows // (4 * SUBLANES)
    return pl.pallas_call(
        fold_kernel,
        out_shape=[
            jax.ShapeDtypeStruct((parts, 4 * SUBLANES, LANES), jnp.bfloat16),
            jax.ShapeDtypeStruct((SUBLANES, LANES), jnp.bfloat16),
        ],
        in_specs=[pl.BlockSpec(memory_space=pltpu.HBM)],
        out_specs=[pl.BlockSpec(memory_space=pltpu.VMEM)] * 2,
        scratch_shapes=[pltpu.VMEM((size, size), jnp.bfloat16), pltpu.SemaphoreType.DMA((count,))],
        compiler_params=pltpu.CompilerParams(vmem_limit_bytes=HIGH),
        cost_estimate=pl.CostEstimate(flops=2 * size * size, bytes_accessed=3 * size * size, transcendentals=0),
        name="fold",
    )(tensor)


def advect_kernel(flags_ref, courant_ref, before_ref, here_ref, after_ref, out_ref):
    nodes = here_ref.shape[0]
    width = here_ref.shape[1] // out_ref.shape[0]
    row = lax.broadcasted_iota(jnp.int32, (nodes, 1), 0)
    flag = jnp.zeros((nodes, 1), jnp.int32)
    rate = jnp.zeros((nodes, 1), jnp.float32)
    for r in range(nodes):
        flag = jnp.where(row == r, flags_ref[r], flag)
        rate = jnp.where(row == r, courant_ref[r], rate)
    upward = jnp.broadcast_to(flag, (nodes, width)) == 1
    for d in range(out_ref.shape[0]):
        start, stop = d * width, (d + 1) * width
        last = d == out_ref.shape[0] - 1
        before = before_ref[...] if d == 0 else here_ref[:, start - LANES : start]
        after = after_ref[...] if last else here_ref[:, stop : stop + LANES]
        field = here_ref[:, start:stop].astype(jnp.float32)
        line = jnp.concatenate([before.astype(jnp.float32), field, after.astype(jnp.float32)], axis=1)
        left = pltpu.roll(line, 1, axis=1)[:, LANES : LANES + width]
        right = pltpu.roll(line, width + 2 * LANES - 1, axis=1)[:, LANES : LANES + width]
        neighbour = jnp.where(upward, left, right)
        moved = (field - rate * (field - neighbour)).astype(jnp.bfloat16)
        for t in range(width // LANES):
            out_ref[d, t * nodes : (t + 1) * nodes, :] = moved[:, t * LANES : (t + 1) * LANES]


def advect(density, flags, courant, parts, spare):
    nodes, cells = density.shape
    width = cells // parts
    wide = GROUP * width // LANES
    lines = cells // LANES
    rows = nodes * width // LANES
    return pl.pallas_call(
        advect_kernel,
        grid=(parts // GROUP,),
        out_shape=jax.ShapeDtypeStruct((parts, rows + spare, LANES), jnp.bfloat16),
        in_specs=[
            pl.BlockSpec(memory_space=pltpu.SMEM),
            pl.BlockSpec(memory_space=pltpu.SMEM),
            pl.BlockSpec((nodes, LANES), lambda i: (0, (i * wide + lines - 1) % lines)),
            pl.BlockSpec((nodes, GROUP * width), lambda i: (0, i)),
            pl.BlockSpec((nodes, LANES), lambda i: (0, ((i + 1) * wide) % lines)),
        ],
        out_specs=pl.BlockSpec((GROUP, rows, LANES), lambda i: (i, 0, 0)),
        compiler_params=pltpu.CompilerParams(vmem_limit_bytes=HIGH),
        cost_estimate=pl.CostEstimate(flops=4 * nodes * cells, bytes_accessed=4 * nodes * cells, transcendentals=0),
        name="advect",
    )(flags, courant, density, density, density)


def pick_kernel(owner_ref, pieces_hbm, extra_ref, _, out_hbm, chosen_ref, spread_ref, in_sems, sems):
    half = owner_ref.shape[0] // 2
    batch, rows = spread_ref.shape[0], spread_ref.shape[1]
    first = out_hbm.shape[1] - rows
    reads = []
    for m in range(2 * half):
        reads.append(pltpu.make_async_copy(pieces_hbm.at[owner_ref[m]], chosen_ref.at[m], in_sems.at[m]))
        reads[m].start()
    for read in reads:
        read.wait()
    extra = extra_ref[...]
    for d in range(batch):
        core, z, y = d % 2, d // 2 % 4, d // 8 % 4
        quarter = (y if core else z) * SUBLANES
        for s in range(half):
            part = chosen_ref[core * half + s, quarter : quarter + SUBLANES, :]
            spread_ref[d, s * SUBLANES : (s + 1) * SUBLANES, :] = part
        spread_ref[d, half * SUBLANES : (half + 1) * SUBLANES, :] = extra
    writes = []
    for b in range(out_hbm.shape[0] // batch):
        target = out_hbm.at[pl.ds(b * batch, batch), pl.ds(first, rows), :]
        writes.append(pltpu.make_async_copy(spread_ref, target, sems.at[b]))
    for write in writes:
        write.start()
    for write in writes:
        write.wait()


def pick(owner, pieces, extra, moved, spare, batch=32):
    parts = pieces.shape[0]
    return pl.pallas_call(
        pick_kernel,
        out_shape=jax.ShapeDtypeStruct(moved.shape, moved.dtype),
        in_specs=[
            pl.BlockSpec(memory_space=pltpu.SMEM),
            pl.BlockSpec(memory_space=pl.ANY),
            pl.BlockSpec(memory_space=pltpu.VMEM),
            pl.BlockSpec(memory_space=pl.ANY),
        ],
        out_specs=pl.BlockSpec(memory_space=pl.ANY),
        scratch_shapes=[
            pltpu.VMEM((owner.shape[0], *pieces.shape[1:]), jnp.bfloat16),
            pltpu.VMEM((batch, spare, LANES), jnp.bfloat16),
            pltpu.SemaphoreType.DMA((owner.shape[0],)),
            pltpu.SemaphoreType.DMA((parts // batch,)),
        ],
        input_output_aliases={3: 0},
        compiler_params=pltpu.CompilerParams(vmem_limit_bytes=HIGH),
        cost_estimate=pl.CostEstimate(flops=0, bytes_accessed=parts * spare * LANES * 2, transcendentals=0),
        name="pick",
    )(owner, pieces, extra, moved)


def unpack_kernel(owner_ref, arrived, near_ref, e_ref):
    end = arrived.shape[1] - SUBLANES
    near_ref[...] = arrived[:, end - near_ref.shape[1] : end, :]
    for m in range(e_ref.shape[0]):
        e_ref[m] = arrived[owner_ref[m], end:, :]


def unpack(owner, arrived, rows):
    slots = owner.shape[0]
    parts = arrived.shape[0]
    return pl.pallas_call(
        unpack_kernel,
        out_shape=[
            jax.ShapeDtypeStruct((parts, rows, LANES), jnp.bfloat16),
            jax.ShapeDtypeStruct((slots, SUBLANES, LANES), jnp.bfloat16),
        ],
        in_specs=[pl.BlockSpec(memory_space=pltpu.SMEM), pl.BlockSpec(memory_space=pltpu.VMEM)],
        out_specs=[pl.BlockSpec(memory_space=pltpu.VMEM)] * 2,
        compiler_params=pltpu.CompilerParams(vmem_limit_bytes=LIMIT),
        cost_estimate=pl.CostEstimate(flops=0, bytes_accessed=4 * parts * rows * LANES, transcendentals=0),
        name="unpack",
    )(owner, arrived)


def transform_kernel(tile, s_ref, x_ref, c_hbm, c_ref, sems):
    parts = x_ref.shape[0]
    nodes = s_ref.shape[1] // parts
    writes = []
    for n in range(c_ref.shape[1] // tile):
        lines = range(n * tile // LANES * nodes, (n + 1) * tile // LANES * nodes, nodes)
        columns = [x_ref[:, t : t + nodes, :].reshape(parts * nodes, LANES) for t in lines]
        block = jnp.concatenate(columns, axis=1)
        cells = pl.ds(n * tile, tile)
        c_ref[:, cells] = jnp.dot(s_ref[...], block, preferred_element_type=jnp.float32).astype(jnp.bfloat16)
        writes.append(pltpu.make_async_copy(c_ref.at[:, cells], c_hbm.at[:, cells], sems.at[n]))
        writes[n].start()
    for write in writes:
        write.wait()


def transform(spectral, arrived, width, tile=512):
    size = spectral.shape[0]
    return pl.pallas_call(
        functools.partial(transform_kernel, tile),
        out_shape=[jax.ShapeDtypeStruct((size, width), jnp.bfloat16)] * 2,
        in_specs=[pl.BlockSpec(memory_space=pltpu.VMEM)] * 2,
        out_specs=[pl.BlockSpec(memory_space=pl.ANY), pl.BlockSpec(memory_space=pltpu.VMEM)],
        scratch_shapes=[pltpu.SemaphoreType.DMA((width // tile,))],
        compiler_params=pltpu.CompilerParams(vmem_limit_bytes=LIMIT),
        cost_estimate=pl.CostEstimate(
            flops=2 * size * size * width, bytes_accessed=6 * size * width, transcendentals=0
        ),
        name="transform",
    )(spectral, arrived)


def quadratic_kernel(pairs, tile, e_ref, c_ref, *refs):
    sources, (out_ref, left_ref, item_ref) = refs[: len(pairs)], refs[-3:]
    size, width = c_ref.shape
    halves = BLOCK // LANES
    run = BLOCK // SUBLANES
    half = e_ref.shape[0] // 2
    above = above_pairs(size // BLOCK)
    row = lax.broadcasted_iota(jnp.int32, (BLOCK, BLOCK), 0)
    col = lax.broadcasted_iota(jnp.int32, (BLOCK, BLOCK), 1)
    factor = 1.0 / math.sqrt(size)
    here = lax.axis_index("dev")
    if len(refs) > len(pairs) + 3:
        out_ref[...] = refs[len(pairs)][...]
    else:
        out_ref[...] = jnp.zeros_like(out_ref)

    def put(at, both, i, j, place):
        left_ref[at] = jnp.concatenate(both, axis=0)
        for side, value in enumerate((i, j, place)):
            item_ref[side, at] = value

    items = jnp.int32(0)
    for source, (mine, k) in zip(sources, pairs):
        core = here % 2 if mine else 1 - here % 2
        quarter = (jnp.where(core == 0, here // 2, here // 8) + 4 - k) % 4
        place = core * half
        full = len(above) // 2

        def block(s, b, source=source):
            panels = []
            for part in range(halves):
                first = (b * halves + part) * run
                lines = source[first : first + run, s * SUBLANES : (s + 1) * SUBLANES, :]
                panels.append(lines.reshape(BLOCK, LANES))
            return jnp.concatenate(panels, axis=1)

        def choose(table, quarter=quarter):
            value = table[0]
            for at in range(1, len(table)):
                value = jnp.where(quarter == at, table[at], value)
            return value

        @pl.when(quarter < full)
        def _(block=block, choose=choose, place=place, items=items):
            for b in range(2):
                i, j = (choose([above[2 * q + b][side] for q in range(full)]) for side in range(2))
                put(items + b, [block(s, b) for s in range(half)], i, j, place)

        @pl.when(quarter == full)
        def _(block=block, place=place, items=items):
            for b in range(2):
                packed = [block(s, b).astype(jnp.float32) for s in range(half)]
                upper = [jnp.where(row <= col, x, 0.0).astype(jnp.bfloat16) for x in packed]
                lower = []
                for s, x in enumerate(packed):
                    values = [e_ref[place + s, pl.ds(b * halves + part, 1), :] for part in range(halves)]
                    line = jnp.concatenate(values, axis=1).astype(jnp.float32)
                    whole = jnp.where(row > col, x, jnp.where(row == col, line, 0.0))
                    lower.append(whole.astype(jnp.bfloat16))
                put(items + 2 * b, upper, 2 * b, 2 * b, place)
                put(items + 2 * b + 1, lower, 2 * b + 1, 2 * b + 1, place)

        items = items + jnp.where(quarter == full, 4, 2)

    def add(at):
        i, j, place = (item_ref[side, at] for side in range(3))
        left = pl.ds(pl.multiple_of(i * BLOCK, BLOCK), BLOCK)
        right = pl.ds(pl.multiple_of(j * BLOCK, BLOCK), BLOCK)
        for first in range(0, width, tile):
            cells = slice(first, first + tile)
            image = jnp.dot(left_ref[at], c_ref[right, cells], preferred_element_type=jnp.float32)
            weight = c_ref[left, cells].astype(jnp.float32)
            for s in range(half):
                term = image[s * BLOCK : (s + 1) * BLOCK] * weight
                line = jnp.sum(jnp.sum(term.reshape(run, SUBLANES, tile), axis=0), axis=0, keepdims=True)
                out_ref[pl.ds(place + s, 1), cells] += line * factor

    @pl.loop(0, items // 2)
    def _(at):
        add(2 * at)
        add(2 * at + 1)


def quadratic(pairs, sources, diagonals, coeffs, before=None, tile=512):
    size, width = coeffs.shape
    slots = diagonals.shape[0]
    args = [diagonals, coeffs, *sources] + ([] if before is None else [before])
    return pl.pallas_call(
        functools.partial(quadratic_kernel, pairs, tile),
        out_shape=jax.ShapeDtypeStruct((slots, width), jnp.float32),
        in_specs=[pl.BlockSpec(memory_space=pltpu.VMEM)] * len(args),
        out_specs=pl.BlockSpec(memory_space=pltpu.VMEM),
        scratch_shapes=[
            pltpu.VMEM((2 * len(pairs) + 4, slots // 2 * BLOCK, BLOCK), jnp.bfloat16),
            pltpu.SMEM((3, 2 * len(pairs) + 4), jnp.int32),
        ],
        compiler_params=pltpu.CompilerParams(vmem_limit_bytes=LIMIT),
        cost_estimate=pl.CostEstimate(
            flops=len(pairs) * size * size * width * 5 // 16, bytes_accessed=2 * size * width, transcendentals=0
        ),
        name="quadratic",
    )(*args)


def exchange(x):
    return lax.all_to_all(x, "dev", split_axis=0, concat_axis=0, tiled=True)


def shift(parts, k):
    pairs = []
    for d in range(parts):
        step = 8 if d % 2 else 2
        at = d // step % 4
        pairs.append((d, d + ((at + k) % 4 - at) * step))
    return pairs


def local(parts, density, flags, courant, spectral, tensor, owner):
    half = owner.shape[0] // 2
    width = density.shape[1] // parts
    spare = (half + 1) * SUBLANES
    folded, extra = fold(tensor)
    pieces = exchange(folded)
    moved = advect(density, flags, courant, parts, spare)
    arrived = exchange(pick(owner, pieces, extra, moved, spare))
    first, diagonals = unpack(owner, arrived, half * SUBLANES)
    pair = [(d, d ^ 1) for d in range(parts)]
    hops = (1, 2, 3)
    near = [lax.ppermute(first, "dev", shift(parts, k)) for k in hops]
    other = lax.ppermute(first, "dev", pair)
    result, coeffs = transform(spectral, arrived, width)
    begun = quadratic([(True, 0), (False, 0)], [first, other], diagonals, coeffs)
    *near, begun = lax.optimization_barrier((*near, begun))
    far = [lax.ppermute(x, "dev", pair) for x in near]
    own = quadratic([(True, k) for k in hops], near, diagonals, coeffs, begun)
    return (result, quadratic([(False, k) for k in hops], far, diagonals, coeffs, own))


def solution(mesh):
    in_specs = (P("dev", None), P("dev"), P("dev"), P(), P("dev", None, None), P())
    out_specs = (P(None, "dev"), P(None, "dev"))

    def step(*args):
        return local(mesh.shape["dev"], *args)

    return jax.shard_map(step, mesh=mesh, in_specs=in_specs, out_specs=out_specs, check_vma=False)
```

```python
import functools
import math

import jax
import jax.numpy as jnp
from jax import lax
from jax.experimental import pallas as pl
from jax.experimental.pallas import tpu as pltpu
from jax.sharding import PartitionSpec as P

BLOCK = 256
LANES = 128
GROUP = 8
SUBLANES = 8
LIMIT = 24 << 20
HIGH = 63 << 20


def fold_kernel(t_hbm, u_ref, e_ref, t_ref, sems):
    count = t_ref.shape[0] // BLOCK
    halves = BLOCK // LANES
    copies = []
    for i in range(count):
        rows = pl.ds(i * BLOCK, BLOCK)
        copies.append(pltpu.make_async_copy(t_hbm.at[0, rows, :], t_ref.at[rows, :], sems.at[i]))
        copies[i].start()

    def load(i, j):
        return t_ref[pl.ds(i * BLOCK, BLOCK), pl.ds(j * BLOCK, BLOCK)].astype(jnp.float32)

    def store(at, block):
        block = block.astype(jnp.bfloat16)
        for half in range(halves):
            quarter, run = divmod(at * halves + half, 4)
            lines = block[:, half * LANES : (half + 1) * LANES].reshape(run_length, SUBLANES, LANES)
            u_ref[pl.ds(run * run_length, run_length), pl.ds(quarter * SUBLANES, SUBLANES), :] = lines

    run_length = BLOCK // SUBLANES
    row = lax.broadcasted_iota(jnp.int32, (BLOCK, BLOCK), 0)
    col = lax.broadcasted_iota(jnp.int32, (BLOCK, BLOCK), 1)
    above = above_pairs(count)
    e_ref[...] = jnp.zeros_like(e_ref)
    for j in range(count):
        copies[j].wait()
        for i in range(j):
            store(above.index((i, j)), load(i, j) + load(j, i).T)
        if j % 2 == 1:
            upper, lower = load(j - 1, j - 1), load(j, j)
            packed = jnp.where(row < col, upper + upper.T, jnp.where(row == col, upper, lower + lower.T))
            store(len(above) + j // 2, packed)
            line = jnp.sum(jnp.where(row == col, lower, 0.0), axis=0, keepdims=True).astype(jnp.bfloat16)
            for half in range(halves):
                e_ref[pl.ds(j // 2 * halves + half, 1), :] = line[:, half * LANES : (half + 1) * LANES]


def above_pairs(count):
    return [(i, j) for j in range(count) for i in range(j)]


def fold(tensor):
    size = tensor.shape[1]
    count = size // BLOCK
    rows = (len(above_pairs(count)) + count // 2) * BLOCK * (BLOCK // LANES)
    parts = rows // (4 * SUBLANES)
    return pl.pallas_call(
        fold_kernel,
        out_shape=[
            jax.ShapeDtypeStruct((parts, 4 * SUBLANES, LANES), jnp.bfloat16),
            jax.ShapeDtypeStruct((SUBLANES, LANES), jnp.bfloat16),
        ],
        in_specs=[pl.BlockSpec(memory_space=pltpu.HBM)],
        out_specs=[pl.BlockSpec(memory_space=pltpu.VMEM)] * 2,
        scratch_shapes=[pltpu.VMEM((size, size), jnp.bfloat16), pltpu.SemaphoreType.DMA((count,))],
        compiler_params=pltpu.CompilerParams(vmem_limit_bytes=HIGH),
        cost_estimate=pl.CostEstimate(flops=2 * size * size, bytes_accessed=3 * size * size, transcendentals=0),
        name="fold",
    )(tensor)


def advect_kernel(flags_ref, courant_ref, before_ref, here_ref, after_ref, out_ref):
    nodes = here_ref.shape[0]
    width = here_ref.shape[1] // out_ref.shape[0]
    row = lax.broadcasted_iota(jnp.int32, (nodes, 1), 0)
    flag = jnp.zeros((nodes, 1), jnp.int32)
    rate = jnp.zeros((nodes, 1), jnp.float32)
    for r in range(nodes):
        flag = jnp.where(row == r, flags_ref[r], flag)
        rate = jnp.where(row == r, courant_ref[r], rate)
    upward = jnp.broadcast_to(flag, (nodes, width)) == 1
    for d in range(out_ref.shape[0]):
        start, stop = d * width, (d + 1) * width
        last = d == out_ref.shape[0] - 1
        before = before_ref[...] if d == 0 else here_ref[:, start - LANES : start]
        after = after_ref[...] if last else here_ref[:, stop : stop + LANES]
        field = here_ref[:, start:stop].astype(jnp.float32)
        line = jnp.concatenate([before.astype(jnp.float32), field, after.astype(jnp.float32)], axis=1)
        left = pltpu.roll(line, 1, axis=1)[:, LANES : LANES + width]
        right = pltpu.roll(line, width + 2 * LANES - 1, axis=1)[:, LANES : LANES + width]
        neighbour = jnp.where(upward, left, right)
        moved = (field - rate * (field - neighbour)).astype(jnp.bfloat16)
        for t in range(width // LANES):
            out_ref[d, t * nodes : (t + 1) * nodes, :] = moved[:, t * LANES : (t + 1) * LANES]


def advect(density, flags, courant, parts, spare):
    nodes, cells = density.shape
    width = cells // parts
    wide = GROUP * width // LANES
    lines = cells // LANES
    rows = nodes * width // LANES
    return pl.pallas_call(
        advect_kernel,
        grid=(parts // GROUP,),
        out_shape=jax.ShapeDtypeStruct((parts, rows + spare, LANES), jnp.bfloat16),
        in_specs=[
            pl.BlockSpec(memory_space=pltpu.SMEM),
            pl.BlockSpec(memory_space=pltpu.SMEM),
            pl.BlockSpec((nodes, LANES), lambda i: (0, (i * wide + lines - 1) % lines)),
            pl.BlockSpec((nodes, GROUP * width), lambda i: (0, i)),
            pl.BlockSpec((nodes, LANES), lambda i: (0, ((i + 1) * wide) % lines)),
        ],
        out_specs=pl.BlockSpec((GROUP, rows, LANES), lambda i: (i, 0, 0)),
        compiler_params=pltpu.CompilerParams(vmem_limit_bytes=HIGH),
        cost_estimate=pl.CostEstimate(flops=4 * nodes * cells, bytes_accessed=4 * nodes * cells, transcendentals=0),
        name="advect",
    )(flags, courant, density, density, density)


def pick_kernel(owner_ref, pieces_ref, extra_ref, _, out_hbm, spread_ref, sems):
    half = owner_ref.shape[0] // 2
    batch, rows = spread_ref.shape[0], spread_ref.shape[1]
    first = out_hbm.shape[1] - rows
    chosen = [pieces_ref[owner_ref[m]] for m in range(2 * half)]
    extra = extra_ref[...]
    for d in range(batch):
        core, z, y = d % 2, d // 2 % 4, d // 8 % 4
        quarter = (y if core else z) * SUBLANES
        for s in range(half):
            part = chosen[core * half + s][quarter : quarter + SUBLANES, :]
            spread_ref[d, s * SUBLANES : (s + 1) * SUBLANES, :] = part
        spread_ref[d, half * SUBLANES : (half + 1) * SUBLANES, :] = extra
    writes = []
    for b in range(out_hbm.shape[0] // batch):
        target = out_hbm.at[pl.ds(b * batch, batch), pl.ds(first, rows), :]
        writes.append(pltpu.make_async_copy(spread_ref, target, sems.at[b]))
    for write in writes:
        write.start()
    for write in writes:
        write.wait()


def pick(owner, pieces, extra, moved, spare, batch=32):
    parts = pieces.shape[0]
    return pl.pallas_call(
        pick_kernel,
        out_shape=jax.ShapeDtypeStruct(moved.shape, moved.dtype),
        in_specs=[
            pl.BlockSpec(memory_space=pltpu.SMEM),
            pl.BlockSpec(memory_space=pltpu.VMEM),
            pl.BlockSpec(memory_space=pltpu.VMEM),
            pl.BlockSpec(memory_space=pl.ANY),
        ],
        out_specs=pl.BlockSpec(memory_space=pl.ANY),
        scratch_shapes=[
            pltpu.VMEM((batch, spare, LANES), jnp.bfloat16),
            pltpu.SemaphoreType.DMA((parts // batch,)),
        ],
        input_output_aliases={3: 0},
        compiler_params=pltpu.CompilerParams(vmem_limit_bytes=HIGH),
        cost_estimate=pl.CostEstimate(flops=0, bytes_accessed=parts * spare * LANES * 2, transcendentals=0),
        name="pick",
    )(owner, pieces, extra, moved)


def unpack_kernel(owner_ref, arrived, near_ref, e_ref):
    end = arrived.shape[1] - SUBLANES
    near_ref[...] = arrived[:, end - near_ref.shape[1] : end, :]
    for m in range(e_ref.shape[0]):
        e_ref[m] = arrived[owner_ref[m], end:, :]


def unpack(owner, arrived, rows):
    slots = owner.shape[0]
    parts = arrived.shape[0]
    return pl.pallas_call(
        unpack_kernel,
        out_shape=[
            jax.ShapeDtypeStruct((parts, rows, LANES), jnp.bfloat16),
            jax.ShapeDtypeStruct((slots, SUBLANES, LANES), jnp.bfloat16),
        ],
        in_specs=[pl.BlockSpec(memory_space=pltpu.SMEM), pl.BlockSpec(memory_space=pltpu.VMEM)],
        out_specs=[pl.BlockSpec(memory_space=pltpu.VMEM)] * 2,
        compiler_params=pltpu.CompilerParams(vmem_limit_bytes=LIMIT),
        cost_estimate=pl.CostEstimate(flops=0, bytes_accessed=4 * parts * rows * LANES, transcendentals=0),
        name="unpack",
    )(owner, arrived)


def transform_kernel(tile, s_ref, x_ref, c_hbm, c_ref, sems):
    parts = x_ref.shape[0]
    nodes = s_ref.shape[1] // parts
    writes = []
    for n in range(c_ref.shape[1] // tile):
        lines = range(n * tile // LANES * nodes, (n + 1) * tile // LANES * nodes, nodes)
        columns = [x_ref[:, t : t + nodes, :].reshape(parts * nodes, LANES) for t in lines]
        block = jnp.concatenate(columns, axis=1)
        cells = pl.ds(n * tile, tile)
        c_ref[:, cells] = jnp.dot(s_ref[...], block, preferred_element_type=jnp.float32).astype(jnp.bfloat16)
        writes.append(pltpu.make_async_copy(c_ref.at[:, cells], c_hbm.at[:, cells], sems.at[n]))
        writes[n].start()
    for write in writes:
        write.wait()


def transform(spectral, arrived, width, tile=512):
    size = spectral.shape[0]
    return pl.pallas_call(
        functools.partial(transform_kernel, tile),
        out_shape=[jax.ShapeDtypeStruct((size, width), jnp.bfloat16)] * 2,
        in_specs=[pl.BlockSpec(memory_space=pltpu.VMEM)] * 2,
        out_specs=[pl.BlockSpec(memory_space=pl.ANY), pl.BlockSpec(memory_space=pltpu.VMEM)],
        scratch_shapes=[pltpu.SemaphoreType.DMA((width // tile,))],
        compiler_params=pltpu.CompilerParams(vmem_limit_bytes=LIMIT),
        cost_estimate=pl.CostEstimate(
            flops=2 * size * size * width, bytes_accessed=6 * size * width, transcendentals=0
        ),
        name="transform",
    )(spectral, arrived)


def quadratic_kernel(pairs, tile, e_ref, c_ref, *refs):
    sources, (out_ref, left_ref, item_ref) = refs[: len(pairs)], refs[-3:]
    size, width = c_ref.shape
    halves = BLOCK // LANES
    run = BLOCK // SUBLANES
    half = e_ref.shape[0] // 2
    above = above_pairs(size // BLOCK)
    row = lax.broadcasted_iota(jnp.int32, (BLOCK, BLOCK), 0)
    col = lax.broadcasted_iota(jnp.int32, (BLOCK, BLOCK), 1)
    factor = 1.0 / math.sqrt(size)
    here = lax.axis_index("dev")
    if len(refs) > len(pairs) + 3:
        out_ref[...] = refs[len(pairs)][...]
    else:
        out_ref[...] = jnp.zeros_like(out_ref)

    def put(at, both, i, j, place):
        left_ref[at] = jnp.concatenate(both, axis=0)
        for side, value in enumerate((i, j, place)):
            item_ref[side, at] = value

    items = jnp.int32(0)
    for source, (mine, k) in zip(sources, pairs):
        core = here % 2 if mine else 1 - here % 2
        quarter = (jnp.where(core == 0, here // 2, here // 8) + 4 - k) % 4
        place = core * half
        full = len(above) // 2

        def block(s, b, source=source):
            panels = []
            for part in range(halves):
                first = (b * halves + part) * run
                lines = source[first : first + run, s * SUBLANES : (s + 1) * SUBLANES, :]
                panels.append(lines.reshape(BLOCK, LANES))
            return jnp.concatenate(panels, axis=1)

        def choose(table, quarter=quarter):
            value = table[0]
            for at in range(1, len(table)):
                value = jnp.where(quarter == at, table[at], value)
            return value

        @pl.when(quarter < full)
        def _(block=block, choose=choose, place=place, items=items):
            for b in range(2):
                i, j = (choose([above[2 * q + b][side] for q in range(full)]) for side in range(2))
                put(items + b, [block(s, b) for s in range(half)], i, j, place)

        @pl.when(quarter == full)
        def _(block=block, place=place, items=items):
            for b in range(2):
                packed = [block(s, b).astype(jnp.float32) for s in range(half)]
                upper = [jnp.where(row <= col, x, 0.0).astype(jnp.bfloat16) for x in packed]
                lower = []
                for s, x in enumerate(packed):
                    values = [e_ref[place + s, pl.ds(b * halves + part, 1), :] for part in range(halves)]
                    line = jnp.concatenate(values, axis=1).astype(jnp.float32)
                    whole = jnp.where(row > col, x, jnp.where(row == col, line, 0.0))
                    lower.append(whole.astype(jnp.bfloat16))
                put(items + 2 * b, upper, 2 * b, 2 * b, place)
                put(items + 2 * b + 1, lower, 2 * b + 1, 2 * b + 1, place)

        items = items + jnp.where(quarter == full, 4, 2)

    def add(at):
        i, j, place = (item_ref[side, at] for side in range(3))
        left = pl.ds(pl.multiple_of(i * BLOCK, BLOCK), BLOCK)
        right = pl.ds(pl.multiple_of(j * BLOCK, BLOCK), BLOCK)
        for first in range(0, width, tile):
            cells = slice(first, first + tile)
            image = jnp.dot(left_ref[at], c_ref[right, cells], preferred_element_type=jnp.float32)
            weight = c_ref[left, cells].astype(jnp.float32)
            for s in range(half):
                term = image[s * BLOCK : (s + 1) * BLOCK] * weight
                line = jnp.sum(jnp.sum(term.reshape(run, SUBLANES, tile), axis=0), axis=0, keepdims=True)
                out_ref[pl.ds(place + s, 1), cells] += line * factor

    @pl.loop(0, items // 2)
    def _(at):
        add(2 * at)
        add(2 * at + 1)


def quadratic(pairs, sources, diagonals, coeffs, before=None, tile=512):
    size, width = coeffs.shape
    slots = diagonals.shape[0]
    args = [diagonals, coeffs, *sources] + ([] if before is None else [before])
    return pl.pallas_call(
        functools.partial(quadratic_kernel, pairs, tile),
        out_shape=jax.ShapeDtypeStruct((slots, width), jnp.float32),
        in_specs=[pl.BlockSpec(memory_space=pltpu.VMEM)] * len(args),
        out_specs=pl.BlockSpec(memory_space=pltpu.VMEM),
        scratch_shapes=[
            pltpu.VMEM((2 * len(pairs) + 4, slots // 2 * BLOCK, BLOCK), jnp.bfloat16),
            pltpu.SMEM((3, 2 * len(pairs) + 4), jnp.int32),
        ],
        compiler_params=pltpu.CompilerParams(vmem_limit_bytes=LIMIT),
        cost_estimate=pl.CostEstimate(
            flops=len(pairs) * size * size * width * 5 // 16, bytes_accessed=2 * size * width, transcendentals=0
        ),
        name="quadratic",
    )(*args)


def exchange(x):
    return lax.all_to_all(x, "dev", split_axis=0, concat_axis=0, tiled=True)


def shift(parts, k):
    pairs = []
    for d in range(parts):
        step = 8 if d % 2 else 2
        at = d // step % 4
        pairs.append((d, d + ((at + k) % 4 - at) * step))
    return pairs


def local(parts, density, flags, courant, spectral, tensor, owner):
    half = owner.shape[0] // 2
    width = density.shape[1] // parts
    spare = (half + 1) * SUBLANES
    folded, extra = fold(tensor)
    pieces = exchange(folded)
    moved = advect(density, flags, courant, parts, spare)
    arrived = exchange(pick(owner, pieces, extra, moved, spare))
    first, diagonals = unpack(owner, arrived, half * SUBLANES)
    pair = [(d, d ^ 1) for d in range(parts)]
    near = {k: lax.ppermute(first, "dev", shift(parts, k)) for k in (2, 1, 3)}
    other = lax.ppermute(first, "dev", pair)
    result, coeffs = transform(spectral, arrived, width)
    sums = quadratic([(True, 0), (False, 0), (True, 3)], [first, other, near[3]], diagonals, coeffs)
    near[1], near[2], near[3], sums = lax.optimization_barrier((near[1], near[2], near[3], sums))
    far = {k: lax.ppermute(near[k], "dev", pair) for k in (1, 2, 3)}
    sums = quadratic([(True, 1), (True, 2)], [near[1], near[2]], diagonals, coeffs, sums)
    rest = (1, 2, 3)
    return (result, quadratic([(False, k) for k in rest], [far[k] for k in rest], diagonals, coeffs, sums))


def solution(mesh):
    in_specs = (P("dev", None), P("dev"), P("dev"), P(), P("dev", None, None), P())
    out_specs = (P(None, "dev"), P(None, "dev"))

    def step(*args):
        return local(mesh.shape["dev"], *args)

    return jax.shard_map(step, mesh=mesh, in_specs=in_specs, out_specs=out_specs, check_vma=False)
```

```python
import functools
import math

import jax
import jax.numpy as jnp
from jax import lax
from jax.experimental import pallas as pl
from jax.experimental.pallas import tpu as pltpu
from jax.sharding import PartitionSpec as P

BLOCK = 256
LANES = 128
GROUP = 8
SUBLANES = 8
LIMIT = 24 << 20
HIGH = 63 << 20


def fold_kernel(t_hbm, u_ref, e_ref, t_ref, sems):
    count = t_ref.shape[0] // BLOCK
    halves = BLOCK // LANES
    copies = []
    for i in range(count):
        rows = pl.ds(i * BLOCK, BLOCK)
        copies.append(pltpu.make_async_copy(t_hbm.at[0, rows, :], t_ref.at[rows, :], sems.at[i]))
        copies[i].start()

    def load(i, j):
        return t_ref[pl.ds(i * BLOCK, BLOCK), pl.ds(j * BLOCK, BLOCK)].astype(jnp.float32)

    def store(at, block):
        block = block.astype(jnp.bfloat16)
        for half in range(halves):
            quarter, run = divmod(at * halves + half, 4)
            lines = block[:, half * LANES : (half + 1) * LANES].reshape(run_length, SUBLANES, LANES)
            u_ref[pl.ds(run * run_length, run_length), pl.ds(quarter * SUBLANES, SUBLANES), :] = lines

    run_length = BLOCK // SUBLANES
    row = lax.broadcasted_iota(jnp.int32, (BLOCK, BLOCK), 0)
    col = lax.broadcasted_iota(jnp.int32, (BLOCK, BLOCK), 1)
    above = above_pairs(count)
    e_ref[...] = jnp.zeros_like(e_ref)
    for j in range(count):
        copies[j].wait()
        for i in range(j):
            store(above.index((i, j)), load(i, j) + load(j, i).T)
        if j % 2 == 1:
            upper, lower = load(j - 1, j - 1), load(j, j)
            packed = jnp.where(row < col, upper + upper.T, jnp.where(row == col, upper, lower + lower.T))
            store(len(above) + j // 2, packed)
            line = jnp.sum(jnp.where(row == col, lower, 0.0), axis=0, keepdims=True).astype(jnp.bfloat16)
            for half in range(halves):
                e_ref[pl.ds(j // 2 * halves + half, 1), :] = line[:, half * LANES : (half + 1) * LANES]


def above_pairs(count):
    return [(i, j) for j in range(count) for i in range(j)]


def fold(tensor):
    size = tensor.shape[1]
    count = size // BLOCK
    rows = (len(above_pairs(count)) + count // 2) * BLOCK * (BLOCK // LANES)
    parts = rows // (4 * SUBLANES)
    return pl.pallas_call(
        fold_kernel,
        out_shape=[
            jax.ShapeDtypeStruct((parts, 4 * SUBLANES, LANES), jnp.bfloat16),
            jax.ShapeDtypeStruct((SUBLANES, LANES), jnp.bfloat16),
        ],
        in_specs=[pl.BlockSpec(memory_space=pltpu.HBM)],
        out_specs=[pl.BlockSpec(memory_space=pltpu.VMEM)] * 2,
        scratch_shapes=[pltpu.VMEM((size, size), jnp.bfloat16), pltpu.SemaphoreType.DMA((count,))],
        compiler_params=pltpu.CompilerParams(vmem_limit_bytes=HIGH),
        cost_estimate=pl.CostEstimate(flops=2 * size * size, bytes_accessed=3 * size * size, transcendentals=0),
        name="fold",
    )(tensor)


def advect_kernel(flags_ref, courant_ref, before_ref, here_ref, after_ref, out_ref):
    nodes = here_ref.shape[0]
    width = here_ref.shape[1] // out_ref.shape[0]
    row = lax.broadcasted_iota(jnp.int32, (nodes, 1), 0)
    flag = jnp.zeros((nodes, 1), jnp.int32)
    rate = jnp.zeros((nodes, 1), jnp.float32)
    for r in range(nodes):
        flag = jnp.where(row == r, flags_ref[r], flag)
        rate = jnp.where(row == r, courant_ref[r], rate)
    upward = jnp.broadcast_to(flag, (nodes, width)) == 1
    for d in range(out_ref.shape[0]):
        start, stop = d * width, (d + 1) * width
        last = d == out_ref.shape[0] - 1
        before = before_ref[...] if d == 0 else here_ref[:, start - LANES : start]
        after = after_ref[...] if last else here_ref[:, stop : stop + LANES]
        field = here_ref[:, start:stop].astype(jnp.float32)
        line = jnp.concatenate([before.astype(jnp.float32), field, after.astype(jnp.float32)], axis=1)
        left = pltpu.roll(line, 1, axis=1)[:, LANES : LANES + width]
        right = pltpu.roll(line, width + 2 * LANES - 1, axis=1)[:, LANES : LANES + width]
        neighbour = jnp.where(upward, left, right)
        moved = (field - rate * (field - neighbour)).astype(jnp.bfloat16)
        for t in range(width // LANES):
            out_ref[d, t * nodes : (t + 1) * nodes, :] = moved[:, t * LANES : (t + 1) * LANES]


def advect(density, flags, courant, parts, spare):
    nodes, cells = density.shape
    width = cells // parts
    wide = GROUP * width // LANES
    lines = cells // LANES
    rows = nodes * width // LANES
    return pl.pallas_call(
        advect_kernel,
        grid=(parts // GROUP,),
        out_shape=jax.ShapeDtypeStruct((parts, rows + spare, LANES), jnp.bfloat16),
        in_specs=[
            pl.BlockSpec(memory_space=pltpu.SMEM),
            pl.BlockSpec(memory_space=pltpu.SMEM),
            pl.BlockSpec((nodes, LANES), lambda i: (0, (i * wide + lines - 1) % lines)),
            pl.BlockSpec((nodes, GROUP * width), lambda i: (0, i)),
            pl.BlockSpec((nodes, LANES), lambda i: (0, ((i + 1) * wide) % lines)),
        ],
        out_specs=pl.BlockSpec((GROUP, rows, LANES), lambda i: (i, 0, 0)),
        compiler_params=pltpu.CompilerParams(vmem_limit_bytes=HIGH),
        cost_estimate=pl.CostEstimate(flops=4 * nodes * cells, bytes_accessed=4 * nodes * cells, transcendentals=0),
        name="advect",
    )(flags, courant, density, density, density)


def pick_kernel(owner_ref, pieces_ref, extra_ref, _, out_hbm, spread_ref, sems):
    half = owner_ref.shape[0] // 2
    batch, rows = spread_ref.shape[0], spread_ref.shape[1]
    first = out_hbm.shape[1] - rows
    chosen = [pieces_ref[owner_ref[m]] for m in range(2 * half)]
    extra = extra_ref[...]
    for d in range(batch):
        core, z, y = d % 2, d // 2 % 4, d // 8 % 4
        quarter = (y if core else z) * SUBLANES
        for s in range(half):
            part = chosen[core * half + s][quarter : quarter + SUBLANES, :]
            spread_ref[d, s * SUBLANES : (s + 1) * SUBLANES, :] = part
        spread_ref[d, half * SUBLANES : (half + 1) * SUBLANES, :] = extra
    writes = []
    for b in range(out_hbm.shape[0] // batch):
        target = out_hbm.at[pl.ds(b * batch, batch), pl.ds(first, rows), :]
        writes.append(pltpu.make_async_copy(spread_ref, target, sems.at[b]))
    for write in writes:
        write.start()
    for write in writes:
        write.wait()


def pick(owner, pieces, extra, moved, spare, batch=32):
    parts = pieces.shape[0]
    return pl.pallas_call(
        pick_kernel,
        out_shape=jax.ShapeDtypeStruct(moved.shape, moved.dtype),
        in_specs=[
            pl.BlockSpec(memory_space=pltpu.SMEM),
            pl.BlockSpec(memory_space=pltpu.VMEM),
            pl.BlockSpec(memory_space=pltpu.VMEM),
            pl.BlockSpec(memory_space=pl.ANY),
        ],
        out_specs=pl.BlockSpec(memory_space=pl.ANY),
        scratch_shapes=[
            pltpu.VMEM((batch, spare, LANES), jnp.bfloat16),
            pltpu.SemaphoreType.DMA((parts // batch,)),
        ],
        input_output_aliases={3: 0},
        compiler_params=pltpu.CompilerParams(vmem_limit_bytes=HIGH),
        cost_estimate=pl.CostEstimate(flops=0, bytes_accessed=parts * spare * LANES * 2, transcendentals=0),
        name="pick",
    )(owner, pieces, extra, moved)


def unpack_kernel(owner_ref, arrived, near_ref, e_ref):
    end = arrived.shape[1] - SUBLANES
    near_ref[...] = arrived[:, end - near_ref.shape[1] : end, :]
    for m in range(e_ref.shape[0]):
        e_ref[m] = arrived[owner_ref[m], end:, :]


def unpack(owner, arrived, rows):
    slots = owner.shape[0]
    parts = arrived.shape[0]
    return pl.pallas_call(
        unpack_kernel,
        out_shape=[
            jax.ShapeDtypeStruct((parts, rows, LANES), jnp.bfloat16),
            jax.ShapeDtypeStruct((slots, SUBLANES, LANES), jnp.bfloat16),
        ],
        in_specs=[pl.BlockSpec(memory_space=pltpu.SMEM), pl.BlockSpec(memory_space=pltpu.VMEM)],
        out_specs=[pl.BlockSpec(memory_space=pltpu.VMEM)] * 2,
        compiler_params=pltpu.CompilerParams(vmem_limit_bytes=LIMIT),
        cost_estimate=pl.CostEstimate(flops=0, bytes_accessed=4 * parts * rows * LANES, transcendentals=0),
        name="unpack",
    )(owner, arrived)


def transform_kernel(tile, s_ref, x_ref, c_hbm, c_ref, sems):
    parts = x_ref.shape[0]
    nodes = s_ref.shape[1] // parts
    writes = []
    for n in range(c_ref.shape[1] // tile):
        lines = range(n * tile // LANES * nodes, (n + 1) * tile // LANES * nodes, nodes)
        columns = [x_ref[:, t : t + nodes, :].reshape(parts * nodes, LANES) for t in lines]
        block = jnp.concatenate(columns, axis=1)
        cells = pl.ds(n * tile, tile)
        c_ref[:, cells] = jnp.dot(s_ref[...], block, preferred_element_type=jnp.float32).astype(jnp.bfloat16)
        writes.append(pltpu.make_async_copy(c_ref.at[:, cells], c_hbm.at[:, cells], sems.at[n]))
        writes[n].start()
    for write in writes:
        write.wait()


def transform(spectral, arrived, width, tile=512):
    size = spectral.shape[0]
    return pl.pallas_call(
        functools.partial(transform_kernel, tile),
        out_shape=[jax.ShapeDtypeStruct((size, width), jnp.bfloat16)] * 2,
        in_specs=[pl.BlockSpec(memory_space=pltpu.VMEM)] * 2,
        out_specs=[pl.BlockSpec(memory_space=pl.ANY), pl.BlockSpec(memory_space=pltpu.VMEM)],
        scratch_shapes=[pltpu.SemaphoreType.DMA((width // tile,))],
        compiler_params=pltpu.CompilerParams(vmem_limit_bytes=LIMIT),
        cost_estimate=pl.CostEstimate(
            flops=2 * size * size * width, bytes_accessed=6 * size * width, transcendentals=0
        ),
        name="transform",
    )(spectral, arrived)


def quadratic_kernel(pairs, tile, e_ref, c_ref, *refs):
    sources, (out_ref, left_ref, item_ref) = refs[: len(pairs)], refs[-3:]
    size, width = c_ref.shape
    halves = BLOCK // LANES
    run = BLOCK // SUBLANES
    half = e_ref.shape[0] // 2
    above = above_pairs(size // BLOCK)
    row = lax.broadcasted_iota(jnp.int32, (BLOCK, BLOCK), 0)
    col = lax.broadcasted_iota(jnp.int32, (BLOCK, BLOCK), 1)
    factor = 1.0 / math.sqrt(size)
    here = lax.axis_index("dev")
    if len(refs) > len(pairs) + 3:
        out_ref[...] = refs[len(pairs)][...]
    else:
        out_ref[...] = jnp.zeros_like(out_ref)

    def put(at, both, i, j, place):
        left_ref[at] = jnp.concatenate(both, axis=0)
        for side, value in enumerate((i, j, place)):
            item_ref[side, at] = value

    items = jnp.int32(0)
    for source, (mine, k) in zip(sources, pairs):
        core = here % 2 if mine else 1 - here % 2
        quarter = (jnp.where(core == 0, here // 2, here // 8) + 4 - k) % 4
        place = core * half
        full = len(above) // 2

        def block(s, b, source=source):
            panels = []
            for part in range(halves):
                first = (b * halves + part) * run
                lines = source[first : first + run, s * SUBLANES : (s + 1) * SUBLANES, :]
                panels.append(lines.reshape(BLOCK, LANES))
            return jnp.concatenate(panels, axis=1)

        def choose(table, quarter=quarter):
            value = table[0]
            for at in range(1, len(table)):
                value = jnp.where(quarter == at, table[at], value)
            return value

        @pl.when(quarter < full)
        def _(block=block, choose=choose, place=place, items=items):
            for b in range(2):
                i, j = (choose([above[2 * q + b][side] for q in range(full)]) for side in range(2))
                put(items + b, [block(s, b) for s in range(half)], i, j, place)

        @pl.when(quarter == full)
        def _(block=block, place=place, items=items):
            for b in range(2):
                packed = [block(s, b).astype(jnp.float32) for s in range(half)]
                upper = [jnp.where(row <= col, x, 0.0).astype(jnp.bfloat16) for x in packed]
                lower = []
                for s, x in enumerate(packed):
                    values = [e_ref[place + s, pl.ds(b * halves + part, 1), :] for part in range(halves)]
                    line = jnp.concatenate(values, axis=1).astype(jnp.float32)
                    whole = jnp.where(row > col, x, jnp.where(row == col, line, 0.0))
                    lower.append(whole.astype(jnp.bfloat16))
                put(items + 2 * b, upper, 2 * b, 2 * b, place)
                put(items + 2 * b + 1, lower, 2 * b + 1, 2 * b + 1, place)

        items = items + jnp.where(quarter == full, 4, 2)

    def add(at):
        i, j, place = (item_ref[side, at] for side in range(3))
        left = pl.ds(pl.multiple_of(i * BLOCK, BLOCK), BLOCK)
        right = pl.ds(pl.multiple_of(j * BLOCK, BLOCK), BLOCK)
        for first in range(0, width, tile):
            cells = slice(first, first + tile)
            image = jnp.dot(left_ref[at], c_ref[right, cells], preferred_element_type=jnp.float32)
            weight = c_ref[left, cells].astype(jnp.float32)
            for s in range(half):
                term = image[s * BLOCK : (s + 1) * BLOCK] * weight
                line = jnp.sum(jnp.sum(term.reshape(run, SUBLANES, tile), axis=0), axis=0, keepdims=True)
                out_ref[pl.ds(place + s, 1), cells] += line * factor

    @pl.loop(0, items // 4)
    def _(at):
        for step in range(4):
            add(4 * at + step)

    @pl.when(items % 4 == 2)
    def _():
        add(items - 2)
        add(items - 1)


def quadratic(pairs, sources, diagonals, coeffs, before=None, tile=512):
    size, width = coeffs.shape
    slots = diagonals.shape[0]
    args = [diagonals, coeffs, *sources] + ([] if before is None else [before])
    return pl.pallas_call(
        functools.partial(quadratic_kernel, pairs, tile),
        out_shape=jax.ShapeDtypeStruct((slots, width), jnp.float32),
        in_specs=[pl.BlockSpec(memory_space=pltpu.VMEM)] * len(args),
        out_specs=pl.BlockSpec(memory_space=pltpu.VMEM),
        scratch_shapes=[
            pltpu.VMEM((2 * len(pairs) + 4, slots // 2 * BLOCK, BLOCK), jnp.bfloat16),
            pltpu.SMEM((3, 2 * len(pairs) + 4), jnp.int32),
        ],
        compiler_params=pltpu.CompilerParams(vmem_limit_bytes=LIMIT),
        cost_estimate=pl.CostEstimate(
            flops=len(pairs) * size * size * width * 5 // 16, bytes_accessed=2 * size * width, transcendentals=0
        ),
        name="quadratic",
    )(*args)


def exchange(x):
    return lax.all_to_all(x, "dev", split_axis=0, concat_axis=0, tiled=True)


def shift(parts, k):
    pairs = []
    for d in range(parts):
        step = 8 if d % 2 else 2
        at = d // step % 4
        pairs.append((d, d + ((at + k) % 4 - at) * step))
    return pairs


def local(parts, density, flags, courant, spectral, tensor, owner):
    half = owner.shape[0] // 2
    width = density.shape[1] // parts
    spare = (half + 1) * SUBLANES
    folded, extra = fold(tensor)
    pieces = exchange(folded)
    moved = advect(density, flags, courant, parts, spare)
    arrived = exchange(pick(owner, pieces, extra, moved, spare))
    first, diagonals = unpack(owner, arrived, half * SUBLANES)
    pair = [(d, d ^ 1) for d in range(parts)]
    near = {k: lax.ppermute(first, "dev", shift(parts, k)) for k in (2, 1, 3)}
    other = lax.ppermute(first, "dev", pair)
    result, coeffs = transform(spectral, arrived, width)
    sums = quadratic([(True, 0), (False, 0), (True, 3)], [first, other, near[3]], diagonals, coeffs)
    near[1], near[2], near[3], sums = lax.optimization_barrier((near[1], near[2], near[3], sums))
    far = {k: lax.ppermute(near[k], "dev", pair) for k in (1, 2, 3)}
    sums = quadratic([(True, 1), (True, 2)], [near[1], near[2]], diagonals, coeffs, sums)
    rest = (1, 2, 3)
    return (result, quadratic([(False, k) for k in rest], [far[k] for k in rest], diagonals, coeffs, sums))


def solution(mesh):
    in_specs = (P("dev", None), P("dev"), P("dev"), P(), P("dev", None, None), P())
    out_specs = (P(None, "dev"), P(None, "dev"))

    def step(*args):
        return local(mesh.shape["dev"], *args)

    return jax.shard_map(step, mesh=mesh, in_specs=in_specs, out_specs=out_specs, check_vma=False)
```
